32 devices in a mesh: prow: 8 (over y, x, core), pcol: 4 (over z).
Axes of the slice: x: 2, y: 2, z: 4, core: 2. Of those that a mesh axis runs over, the one named last changes fastest.
Arguments:
- cov_trail: float32 [1024, 1024], P('prow', 'pcol'), as said below
- factor_panel: bfloat16 [4, 1024, 128], P(None, 'prow'), may hold values from -0.25 to 0.25
- first_level: int32 [8], replicated, may hold values from 0 to 4
- block_slot: int32 [8], replicated, may hold values from 0 to 7, each once
- factor_window: bfloat16 [6, 128, 128], replicated, may hold values from -0.5 to 0.5
- diag_inverse: float32 [4, 128, 128], replicated, as said below
Outputs:
- panel_cov: float32 [4, 1024, 128], P(None, 'prow')
- window_cov: float32 [512, 512], replicated
The draws below stay inside these ranges and needn't reach their ends.
Inputs may be any that keep to these rules, and one draw needn't show every extreme that they name: Trailing block j lies in the pattern of window supernode k exactly when first_level[j] <= k, so the patterns are nested. `block_slot`: a permutation; slot s is held by process row s // 1 and process column s // (8 / pcol size), slots in contiguous blocks. `cov_trail`: symmetric. `diag_inverse`: each block symmetric.
All inputs are finite; a program needn't handle non-finite values.
Results may differ from the reference program's by a relative error of at most 0.0003.
Values may be sent and summed in bfloat16 or wider, within the bound.
A program may use at most 64 MiB of HBM per device.

```python
import jax
import jax.numpy as jnp
from jax import lax

BS = 128
NW = 4
NT = 8
ORDER = 1024
NPAIR = 6


def draw_cov_trail(key, part):
    order_size = NT * BS
    noise = jax.random.normal(key, (order_size, order_size), jnp.float32)
    symmetric = (noise + noise.T) * 0.7071
    row_ids = lax.broadcasted_iota(jnp.int32, (order_size, order_size), 0)
    col_ids = lax.broadcasted_iota(jnp.int32, (order_size, order_size), 1)
    on_diag = jnp.where(row_ids == col_ids, jnp.float32(2.0), jnp.float32(0.0))
    return symmetric + on_diag


def draw_diag_inverse(key, part):
    noise = jax.random.normal(key, (NW, BS, BS), jnp.float32) * 0.01
    symmetric = noise + jnp.swapaxes(noise, 1, 2)
    row_ids = lax.broadcasted_iota(jnp.int32, (NW, BS, BS), 1)
    col_ids = lax.broadcasted_iota(jnp.int32, (NW, BS, BS), 2)
    return symmetric + jnp.where(row_ids == col_ids, jnp.float32(2.0), jnp.float32(0.0))


def set_ends(result, stream_key, low, largest):
    longest = result.shape.index(max(result.shape))
    spots = []
    for shift in (0, 1):
        where = [jax.random.randint(jax.random.fold_in(stream_key, axis), (), 0, length) for axis, length in enumerate(result.shape)]
        where[longest] = (where[longest] + shift) % result.shape[longest]
        spots.append(tuple(where))
    return result.at[spots[0]].set(low).at[spots[1]].set(largest)


def block_levels(stream_key, extent, shards, low, largest):
    loudness = 1.0
    for dim, shards_of in shards:
        draws = jax.random.uniform(jax.random.fold_in(jax.random.fold_in(stream_key, 6), dim), (shards_of,), jnp.float32, low / len(shards), largest / len(shards))
        loudness = loudness * jnp.repeat(jnp.exp(draws), extent[dim] // shards_of).reshape((-1,) + (1,) * (len(extent) - 1 - dim))
    return loudness


def gaussian(own_key, dims, deviation, reach, shards=(), kind=jnp.bfloat16):
    entries = deviation * jax.random.normal(own_key, dims, jnp.float32)
    if shards:
        entries = entries * block_levels(own_key, dims, shards, -0.22, 0.18)
    return jnp.clip(entries, -reach, reach).astype(kind)


def setup_inputs(seed: int = 0) -> dict:
    key_of = jax.random.split(jax.random.key(seed), 7)
    cov_trail = draw_cov_trail(jax.random.fold_in(key_of[6], 71), 0)
    factor_panel = gaussian(key_of[1], (NW, ORDER, BS), (64 * NT) ** -0.5, 0.25, ((1, 8),))
    first_level = set_ends(jax.random.randint(key_of[2], (NT,), 0, NW + 1), jax.random.fold_in(key_of[2], 1), 0, NW).astype(jnp.int32)
    block_slot = jax.random.permutation(key_of[3], NT).astype(jnp.int32)
    factor_window = gaussian(key_of[4], (NPAIR, BS, BS), BS ** -0.5, 0.5)
    diag_inverse = draw_diag_inverse(jax.random.fold_in(key_of[6], 71), 0)
    return {"cov_trail": cov_trail, "factor_panel": factor_panel, "first_level": first_level, "block_slot": block_slot, "factor_window": factor_window, "diag_inverse": diag_inverse}


def pair_index(upper, lower, window_count):
    return lower * window_count - lower * (lower + 1) // 2 + upper - lower - 1


def later_block(window, upper, lower):
    if upper >= lower:
        return window[(upper, lower)]
    return window[(lower, upper)].T


def reference(cov_trail, factor_panel, first_level, block_slot, factor_window, diag_inverse):
    highest = lax.Precision.HIGHEST
    slot_ids = jnp.arange(NT, dtype=jnp.int32)
    level_slot = jnp.sum(jnp.where(block_slot[None, :] == slot_ids[:, None], first_level[None, :], 0), axis=1)
    row_level = jnp.repeat(level_slot, BS)
    columns = {}
    window = {}
    for supernode in range(NW - 1, -1, -1):
        keep_rows = (row_level <= supernode)[:, None]
        panel_full = jnp.where(keep_rows, factor_panel[supernode].astype(jnp.float32), jnp.float32(0.0))
        later_nodes = list(range(supernode + 1, NW))
        window_factor = [factor_window[pair_index(upper, supernode, NW)].astype(jnp.float32) for upper in later_nodes]
        accumulated = jnp.dot(cov_trail, panel_full, precision=highest, preferred_element_type=jnp.float32)
        for place, upper in enumerate(later_nodes):
            accumulated = accumulated + jnp.dot(columns[upper], window_factor[place], precision=highest, preferred_element_type=jnp.float32)
        new_column = jnp.where(keep_rows, -accumulated, jnp.float32(0.0))
        columns[supernode] = new_column
        for upper in later_nodes:
            block_total = jnp.dot(columns[upper].T, panel_full, precision=highest, preferred_element_type=jnp.float32)
            for place, other in enumerate(later_nodes):
                block_total = block_total + jnp.dot(later_block(window, upper, other), window_factor[place], precision=highest, preferred_element_type=jnp.float32)
            window[(upper, supernode)] = -block_total
        diagonal = diag_inverse[supernode] - jnp.dot(panel_full.T, new_column, precision=highest, preferred_element_type=jnp.float32)
        for place, upper in enumerate(later_nodes):
            diagonal = diagonal - jnp.dot(window_factor[place].T, window[(upper, supernode)], precision=highest, preferred_element_type=jnp.float32)
        window[(supernode, supernode)] = diagonal
    panel_cov = jnp.stack([columns[supernode] for supernode in range(NW)])
    block_rows = [jnp.concatenate([later_block(window, upper, other) for other in range(NW)], axis=1) for upper in range(NW)]
    window_cov = jnp.concatenate(block_rows, axis=0)
    return panel_cov, window_cov
```

```python
import functools

import jax
import jax.numpy as jnp
from jax import lax
from jax.experimental import pallas as pl
from jax.experimental.pallas import tpu as pltpu
from jax.sharding import PartitionSpec as P

MESH = pl.DeviceIdType.MESH
F32 = jnp.float32
BF16 = jnp.bfloat16
LANES = (((1,), (1,)), ((), ()))


def pair_index(upper, lower, window_count):
    return lower * window_count - lower * (lower + 1) // 2 + upper - lower - 1


def split(value):
    high = value.astype(BF16)
    return high, (value - high.astype(F32)).astype(BF16)


def dot(left, right):
    return jnp.dot(left, right, preferred_element_type=F32)


def dot2(parts, right):
    rows = parts[0].shape[0]
    both = dot(jnp.concatenate(parts, axis=0), right)
    return both[:rows] + both[rows:]


def dot3(parts, right_high, right_low):
    return dot2(parts, right_high) + dot(parts[0], right_low)


def kernel(
    sizes,
    first_hbm,
    slot_hbm,
    cov_hbm,
    panel_hbm,
    factor_hbm,
    diag_hbm,
    column_ref,
    window_ref,
    first_ref,
    slot_ref,
    cov_ref,
    panels,
    factor_ref,
    diag_ref,
    inverse,
    inverse_t,
    masked,
    partial,
    partial_in,
    product,
    column_in,
    load_sem,
    cov_send,
    cov_recv,
    panel_send,
    panel_fwd,
    panel_recv,
    partial_send,
    partial_recv,
    product_send,
    product_recv,
    column_send,
    column_recv,
    row_send,
    row_fwd,
    row_recv,
):
    n_row, n_col, window_count, block, parts = sizes
    n_chip = n_row // 2
    width = window_count * block
    chunk = width // n_row
    piece = chunk // parts
    cols = cov_ref.shape[2]
    local_blocks = cols // block
    block_count = first_ref.shape[0]
    me = lax.axis_index("prow")
    col = lax.axis_index("pcol")
    core = lax.rem(me, 2)
    chip = me // 2
    partner = chip * 2 + 1 - core

    def remote(src, dst, send, recv, row, column):
        return pltpu.make_async_remote_copy(
            src_ref=src,
            dst_ref=dst,
            send_sem=send,
            recv_sem=recv,
            device_id=(row, column),
            device_id_type=MESH,
        )

    def level_of(slot):
        level = jnp.int32(0)
        for index in range(block_count):
            level = level + jnp.where(slot_ref[index] == slot, first_ref[index], 0)
        return level

    def at(start, size):
        return pl.ds(pl.multiple_of(start, size), size)

    def other_chips():
        return [lax.rem(chip + step, n_chip) for step in range(1, n_chip)]

    def other_cols():
        return [lax.rem(col + step, n_col) for step in range(1, n_col)]

    loads = [
        pltpu.make_async_copy(source, target, load_sem.at[index])
        for index, (source, target) in enumerate(
            (
                (factor_hbm, factor_ref),
                (panel_hbm, panels.at[me]),
                (first_hbm, first_ref),
                (slot_hbm, slot_ref),
                (cov_hbm, cov_ref.at[core]),
                (diag_hbm, diag_ref),
            )
        )
    ]
    for load in loads:
        load.start()
    barrier = pltpu.get_barrier_semaphore()
    for step in range(1, n_row):
        pl.semaphore_signal(
            barrier, inc=1, device_id=(lax.rem(me + step, n_row), col), device_id_type=MESH
        )
    for step in range(1, n_col):
        pl.semaphore_signal(
            barrier, inc=1, device_id=(me, lax.rem(col + step, n_col)), device_id_type=MESH
        )

    loads[0].wait()

    def factor(w, k):
        return factor_ref[pair_index(w, k, window_count)]

    rows_id = lax.broadcasted_iota(jnp.int32, (block, block), 0)
    cols_id = lax.broadcasted_iota(jnp.int32, (block, block), 1)
    eye = jnp.where(rows_id == cols_id, 1.0, 0.0).astype(BF16)
    zero = jnp.zeros((block, block), BF16)
    inv = {}
    for distance in range(1, window_count):
        for k in range(window_count - distance):
            w = k + distance
            value = factor(w, k).astype(F32)
            for v in range(k + 1, w):
                high, low = inv[v, k]
                value = value + dot(factor(w, v), high) + dot(factor(w, v), low)
            value = -value
            inv[w, k] = split(value)
            turned = split(value.T)
            for part in range(2):
                inverse[part, w * block : (w + 1) * block, k * block : (k + 1) * block] = inv[w, k][part]
                inverse[part, k * block : (k + 1) * block, w * block : (w + 1) * block] = zero
                inverse_t[part, k * block : (k + 1) * block, w * block : (w + 1) * block] = turned[part]
                inverse_t[part, w * block : (w + 1) * block, k * block : (k + 1) * block] = zero
    for k in range(window_count):
        here = slice(k * block, (k + 1) * block)
        for target in (inverse, inverse_t):
            target[0, here, here] = eye
            target[1, here, here] = zero

    for load in loads[1:5]:
        load.wait()

    def mask(row, level):
        for k in range(window_count):
            masked[at(row * block, block), k * block : (k + 1) * block] = jnp.where(
                level <= k, panels[row, k].astype(F32), 0.0
            ).astype(BF16)

    turn = jnp.concatenate(
        [
            inverse_t[part, at((2 * target + core) * chunk, chunk), :]
            for part in range(2)
            for target in range(n_chip)
        ],
        axis=0,
    )
    half = width // 2

    def multiply(row, side):
        both = lax.dot_general(turn, masked[at(row * block, block), :], LANES, preferred_element_type=F32)
        return dot3(split(both[:half] + both[half:]), *split(cov_ref[side]))

    own_level = level_of(me)
    mask(me, own_level)
    first_half = multiply(me, core)

    pl.semaphore_wait(barrier, n_row + n_col - 2)

    def cov_copy():
        return remote(cov_ref.at[core], cov_ref.at[core], cov_send.at[0], cov_recv.at[0], partner, col)

    def panel_copy(row, send, target):
        return remote(panels.at[row], panels.at[row], send, panel_recv.at[row], target, col)

    panel_copy(me, panel_fwd.at[chip], partner).start()
    cov_copy().start()
    partner_level = level_of(partner)
    panel_copy(partner, panel_fwd.at[chip], partner).wait_recv()
    mask(partner, partner_level)
    remote(
        cov_ref.at[core], cov_ref.at[1 - core], cov_send.at[0], cov_recv.at[0], partner, col
    ).wait_recv()
    both_halves = first_half + multiply(partner, 1 - core)
    for target in range(n_chip):
        partial[target] = both_halves[target * chunk : (target + 1) * chunk]

    def part_rows(part):
        return slice(part * piece, (part + 1) * piece)

    def partial_copy(source, origin, part, target):
        return remote(
            partial.at[source, part_rows(part)],
            partial_in.at[origin, part_rows(part)],
            partial_send.at[source, part],
            partial_recv.at[origin, part],
            target * 2 + core,
            col,
        )

    for part in range(parts):
        for target in other_chips():
            partial_copy(target, chip, part, target).start()
    for step, target in enumerate(other_chips()):
        panel_copy(me, panel_send.at[step], target * 2 + core).start()

    def product_copy(source, part, step, target):
        return remote(
            product.at[source, part_rows(part)],
            product.at[source, part_rows(part)],
            product_send.at[step, part],
            product_recv.at[source, part],
            me,
            target,
        )

    for part in range(parts):
        total = partial[chip, part_rows(part)]
        for source in other_chips():
            partial_copy(source, source, part, source).wait_recv()
            total = total + partial_in[source, part_rows(part)]
        product[col, part_rows(part)] = total
        for step, target in enumerate(other_cols()):
            product_copy(col, part, step, target).start()

    loads[5].wait()
    mine = at(me * chunk, chunk)
    scaled = []
    for k in range(window_count):
        here = slice(k * block, (k + 1) * block)
        scaled.append(
            dot3((inverse_t[0, mine, here], inverse_t[1, mine, here]), *split(diag_ref[k]))
        )
    scaled = jnp.concatenate(scaled, axis=1)
    for source in other_chips():
        row = source * 2 + core
        panel_copy(row, panel_fwd.at[source], partner).wait_recv()
        panel_copy(row, panel_fwd.at[source], partner).start()
        mask(row, level_of(row))
    for source in other_chips():
        row = source * 2 + 1 - core
        panel_copy(row, panel_fwd.at[source], partner).wait_recv()
        mask(row, level_of(row))

    def column_copy(z, index, part, target, origin):
        return remote(
            product.at[z, part_rows(part), at(index * block, block)],
            column_in.at[origin, part_rows(part)],
            column_send.at[target, part],
            column_recv.at[origin, part],
            target,
            col,
        )

    def row_copy(row, part, send, target):
        here = at(row * chunk + part * piece, piece)
        return remote(window_ref.at[here], window_ref.at[here], send, row_recv.at[row, part], target, col)

    for part in range(parts):
        total = scaled[part_rows(part)]
        for step, z in enumerate([col] + other_cols()):
            if step:
                product_copy(z, part, step - 1, z).wait_recv()
            for index in range(local_blocks):
                slot = z * local_blocks + index

                @pl.when(slot != me)
                def _():
                    column_copy(z, index, part, slot, me).start()

            total = total + dot2(split(product[z, part_rows(part)]), masked[at(z * cols, cols), :])
        window_ref[at(me * chunk + part * piece, piece), :] = dot3(split(total), inverse[0], inverse[1])
        for target in other_chips():
            row_copy(me, part, row_send.at[target, part], target * 2 + core).start()
        row_copy(me, part, row_fwd.at[chip, part], partner).start()

    column_in[me] = product[me // local_blocks, :, at(lax.rem(me, local_blocks) * block, block)]
    for step in range(1, n_row):
        source = lax.rem(me + step, n_row)
        for part in range(parts):
            column_copy(0, 0, part, source, source).wait_recv()
    for k in range(window_count):
        per_block = block // chunk
        value = jnp.concatenate([column_in[k * per_block + index] for index in range(per_block)], axis=0)
        column_ref[k] = jnp.where(own_level <= k, -value.T, 0.0)

    for part in range(parts):
        for source in other_chips():
            forward = row_copy(source * 2 + core, part, row_fwd.at[source, part], partner)
            forward.wait_recv()
            forward.start()
    for part in range(parts):
        for source in range(n_chip):
            row_copy(source * 2 + 1 - core, part, row_fwd.at[source, part], partner).wait_recv()

    cov_copy().wait_send()
    for step in range(n_chip - 1):
        panel_copy(me, panel_send.at[step], partner).wait_send()
    for source in range(n_chip):
        panel_copy(me, panel_fwd.at[source], partner).wait_send()
    for part in range(parts):
        for target in other_chips():
            partial_copy(target, chip, part, target).wait_send()
        for step, target in enumerate(other_cols()):
            product_copy(col, part, step, target).wait_send()
        for step in range(1, n_row):
            column_copy(0, 0, part, lax.rem(me + step, n_row), me).wait_send()
        for target in other_chips():
            row_copy(me, part, row_send.at[target, part], target * 2 + core).wait_send()
        for source in range(n_chip):
            row_copy(me, part, row_fwd.at[source, part], partner).wait_send()


def solution(mesh):
    n_row, n_col = mesh.shape["prow"], mesh.shape["pcol"]

    def shards(cov_trail, factor_panel, first_level, block_slot, factor_window, diag_inverse):
        window_count, block = diag_inverse.shape[0], diag_inverse.shape[-1]
        rows, cols = cov_trail.shape
        width = window_count * block
        chunk = width // n_row
        parts = 2 if chunk % 32 == 0 else 1
        n_chip = n_row // 2
        vmem = pl.BlockSpec(memory_space=pltpu.VMEM)
        hbm = pl.BlockSpec(memory_space=pltpu.MemorySpace.HBM)
        dma = pltpu.SemaphoreType.DMA
        return pl.pallas_call(
            functools.partial(kernel, (n_row, n_col, window_count, block, parts)),
            out_shape=(
                jax.ShapeDtypeStruct((window_count, rows, block), F32),
                jax.ShapeDtypeStruct((width, width), F32),
            ),
            in_specs=[hbm] * 6,
            out_specs=(vmem, vmem),
            scratch_shapes=[
                pltpu.SMEM(first_level.shape, jnp.int32),
                pltpu.SMEM(block_slot.shape, jnp.int32),
                pltpu.VMEM((2, rows, cols), F32),
                pltpu.VMEM((n_row,) + factor_panel.shape, BF16),
                pltpu.VMEM(factor_window.shape, BF16),
                pltpu.VMEM(diag_inverse.shape, F32),
                pltpu.VMEM((2, width, width), BF16),
                pltpu.VMEM((2, width, width), BF16),
                pltpu.VMEM((n_row * rows, width), BF16),
                pltpu.VMEM((n_chip, chunk, cols), F32),
                pltpu.VMEM((n_chip, chunk, cols), F32),
                pltpu.VMEM((n_col, chunk, cols), F32),
                pltpu.VMEM((n_row, chunk, block), F32),
                dma((6,)),
                dma((1,)),
                dma((1,)),
                dma((n_chip,)),
                dma((n_chip,)),
                dma((n_row,)),
                dma((n_chip, parts)),
                dma((n_chip, parts)),
                dma((n_col, parts)),
                dma((n_col, parts)),
                dma((n_row, parts)),
                dma((n_row, parts)),
                dma((n_chip, parts)),
                dma((n_chip, parts)),
                dma((n_row, parts)),
            ],
            compiler_params=pltpu.CompilerParams(
                collective_id=0, has_side_effects=True, vmem_limit_bytes=40 * 1024 * 1024
            ),
        )(
            *(
                pltpu.with_memory_space_constraint(value, pltpu.MemorySpace.HBM)
                for value in (first_level, block_slot, cov_trail, factor_panel, factor_window, diag_inverse)
            )
        )

    return jax.shard_map(
        shards,
        mesh=mesh,
        in_specs=(P("prow", "pcol"), P(None, "prow", None), P(), P(), P(), P()),
        out_specs=(P(None, "prow", None), P()),
        check_vma=False,
    )
```

```python
import functools

import jax
import jax.numpy as jnp
from jax import lax
from jax.experimental import pallas as pl
from jax.experimental.pallas import tpu as pltpu
from jax.sharding import PartitionSpec as P

MESH = pl.DeviceIdType.MESH
F32 = jnp.float32
BF16 = jnp.bfloat16
LANES = (((1,), (1,)), ((), ()))


def pair_index(upper, lower, window_count):
    return lower * window_count - lower * (lower + 1) // 2 + upper - lower - 1


def split(value):
    high = value.astype(BF16)
    return high, (value - high.astype(F32)).astype(BF16)


def dot(left, right):
    return jnp.dot(left, right, preferred_element_type=F32)


def dot2(parts, right):
    rows = parts[0].shape[0]
    both = dot(jnp.concatenate(parts, axis=0), right)
    return both[:rows] + both[rows:]


def dot3(parts, right_high, right_low):
    return dot2(parts, right_high) + dot(parts[0], right_low)


def kernel(
    sizes,
    first_hbm,
    slot_hbm,
    cov_hbm,
    panel_hbm,
    factor_hbm,
    diag_hbm,
    column_ref,
    window_ref,
    first_ref,
    slot_ref,
    cov_ref,
    panels,
    factor_ref,
    diag_ref,
    inverse,
    inverse_t,
    masked,
    partial,
    partial_in,
    product,
    column_in,
    full,
    kept_rows,
    load_sem,
    cov_send,
    cov_recv,
    panel_send,
    panel_fwd,
    panel_recv,
    partial_send,
    partial_recv,
    product_send,
    product_recv,
    column_send,
    column_recv,
    row_send,
    row_fwd,
    row_recv,
):
    n_row, n_col, window_count, block, parts = sizes
    n_chip = n_row // 2
    width = window_count * block
    chunk = width // n_row
    piece = chunk // parts
    cols = cov_ref.shape[2]
    local_blocks = cols // block
    block_count = first_ref.shape[0]
    me = lax.axis_index("prow")
    col = lax.axis_index("pcol")
    core = lax.rem(me, 2)
    chip = me // 2
    partner = chip * 2 + 1 - core

    def remote(src, dst, send, recv, row, column):
        return pltpu.make_async_remote_copy(
            src_ref=src,
            dst_ref=dst,
            send_sem=send,
            recv_sem=recv,
            device_id=(row, column),
            device_id_type=MESH,
        )

    def level_of(slot):
        level = jnp.int32(0)
        for index in range(block_count):
            level = level + jnp.where(slot_ref[index] == slot, first_ref[index], 0)
        return level

    def at(start, size):
        return pl.ds(pl.multiple_of(start, size), size)

    def other_chips():
        return [lax.rem(chip + step, n_chip) for step in range(1, n_chip)]

    def other_cols():
        return [lax.rem(col + step, n_col) for step in range(1, n_col)]

    loads = [
        pltpu.make_async_copy(source, target, load_sem.at[index])
        for index, (source, target) in enumerate(
            (
                (factor_hbm, factor_ref),
                (panel_hbm, panels.at[me]),
                (first_hbm, first_ref),
                (slot_hbm, slot_ref),
                (cov_hbm, cov_ref.at[core]),
                (diag_hbm, diag_ref),
            )
        )
    ]
    for load in loads:
        load.start()
    barrier = pltpu.get_barrier_semaphore()
    for step in range(1, n_row):
        pl.semaphore_signal(
            barrier, inc=1, device_id=(lax.rem(me + step, n_row), col), device_id_type=MESH
        )
    for step in range(1, n_col):
        pl.semaphore_signal(
            barrier, inc=1, device_id=(me, lax.rem(col + step, n_col)), device_id_type=MESH
        )

    loads[0].wait()

    def factor(w, k):
        return factor_ref[pair_index(w, k, window_count)]

    rows_id = lax.broadcasted_iota(jnp.int32, (block, block), 0)
    cols_id = lax.broadcasted_iota(jnp.int32, (block, block), 1)
    eye = jnp.where(rows_id == cols_id, 1.0, 0.0).astype(BF16)
    zero = jnp.zeros((block, block), BF16)
    inv = {}
    for distance in range(1, window_count):
        for k in range(window_count - distance):
            w = k + distance
            value = factor(w, k).astype(F32)
            for v in range(k + 1, w):
                high, low = inv[v, k]
                value = value + dot(factor(w, v), high) + dot(factor(w, v), low)
            value = -value
            inv[w, k] = split(value)
            turned = split(value.T)
            for part in range(2):
                inverse[part, w * block : (w + 1) * block, k * block : (k + 1) * block] = inv[w, k][part]
                inverse[part, k * block : (k + 1) * block, w * block : (w + 1) * block] = zero
                inverse_t[part, k * block : (k + 1) * block, w * block : (w + 1) * block] = turned[part]
                inverse_t[part, w * block : (w + 1) * block, k * block : (k + 1) * block] = zero
    for k in range(window_count):
        here = slice(k * block, (k + 1) * block)
        for target in (inverse, inverse_t):
            target[0, here, here] = eye
            target[1, here, here] = zero

    for load in loads[1:5]:
        load.wait()

    def mask(row, level):
        for k in range(window_count):
            masked[at(row * block, block), k * block : (k + 1) * block] = jnp.where(
                level <= k, panels[row, k].astype(F32), 0.0
            ).astype(BF16)

    turn = jnp.concatenate(
        [
            inverse_t[part, at((2 * target + core) * chunk, chunk), :]
            for part in range(2)
            for target in range(n_chip)
        ],
        axis=0,
    )
    half = width // 2

    def multiply(row, side):
        both = lax.dot_general(turn, masked[at(row * block, block), :], LANES, preferred_element_type=F32)
        return dot3(split(both[:half] + both[half:]), *split(cov_ref[side]))

    own_level = level_of(me)
    mask(me, own_level)
    first_half = multiply(me, core)

    pl.semaphore_wait(barrier, n_row + n_col - 2)

    def cov_copy():
        return remote(cov_ref.at[core], cov_ref.at[core], cov_send.at[0], cov_recv.at[0], partner, col)

    groups = [(0, window_count // 2), (window_count // 2, window_count)]

    def panel_copy(row, group, sems, slot, target):
        first, last = groups[group]
        here = panels.at[row, first:last]
        return remote(here, here, sems.at[slot, group], panel_recv.at[row, group], target, col)

    for group in range(2):
        panel_copy(me, group, panel_fwd, chip, partner).start()
    cov_copy().start()
    for step, target in enumerate(other_chips()):
        panel_copy(me, 0, panel_send, step, target * 2 + core).start()
    partner_level = level_of(partner)
    for group in range(2):
        panel_copy(partner, group, panel_fwd, chip, partner).wait_recv()
    mask(partner, partner_level)
    cov_copy().wait_recv()
    both_halves = first_half + multiply(partner, 1 - core)
    for target in range(n_chip):
        partial[target] = both_halves[target * chunk : (target + 1) * chunk]

    def part_rows(part):
        return slice(part * piece, (part + 1) * piece)

    def partial_copy(source, origin, part, target):
        return remote(
            partial.at[source, part_rows(part)],
            partial_in.at[origin, part_rows(part)],
            partial_send.at[source, part],
            partial_recv.at[origin, part],
            target * 2 + core,
            col,
        )

    for part in range(parts):
        for target in other_chips():
            partial_copy(target, chip, part, target).start()
    for step, target in enumerate(other_chips()):
        panel_copy(me, 1, panel_send, step, target * 2 + core).start()

    def product_copy(source, part, step, target):
        return remote(
            product.at[source, part_rows(part)],
            product.at[source, part_rows(part)],
            product_send.at[step, part],
            product_recv.at[source, part],
            me,
            target,
        )

    for part in range(parts):
        total = partial[chip, part_rows(part)]
        for source in other_chips():
            partial_copy(source, source, part, source).wait_recv()
            total = total + partial_in[source, part_rows(part)]
        product[col, part_rows(part)] = total
        for step, target in enumerate(other_cols()):
            product_copy(col, part, step, target).start()

    loads[5].wait()
    mine = at(me * chunk, chunk)
    scaled = []
    for k in range(window_count):
        here = slice(k * block, (k + 1) * block)
        scaled.append(
            dot3((inverse_t[0, mine, here], inverse_t[1, mine, here]), *split(diag_ref[k]))
        )
    scaled = jnp.concatenate(scaled, axis=1)
    for group in range(2):
        for source in other_chips():
            forward = panel_copy(source * 2 + core, group, panel_fwd, source, partner)
            forward.wait_recv()
            forward.start()
    for source in other_chips():
        row = source * 2 + core
        mask(row, level_of(row))
    for source in other_chips():
        row = source * 2 + 1 - core
        for group in range(2):
            panel_copy(row, group, panel_fwd, source, partner).wait_recv()
        mask(row, level_of(row))

    def column_copy(z, index, part, target, origin):
        return remote(
            product.at[z, part_rows(part), at(index * block, block)],
            column_in.at[origin, part_rows(part)],
            column_send.at[target, part],
            column_recv.at[origin, part],
            target,
            col,
        )

    kept = kept_rows.shape[2] // block
    per_block = block // chunk

    def row_copy(row, part, send, target):
        here = kept_rows.at[row, part_rows(part)]
        return remote(here, here, send, row_recv.at[row, part], target, col)

    def place(row, part):
        first = row // per_block
        for offset in range(kept):
            there = lax.rem(first + offset, window_count)
            window_ref[at(row * chunk + part * piece, piece), at(there * block, block)] = kept_rows[
                row, part_rows(part), offset * block : (offset + 1) * block
            ]

    for part in range(parts):
        total = scaled[part_rows(part)]
        for step, z in enumerate([col] + other_cols()):
            if step:
                product_copy(z, part, step - 1, z).wait_recv()
            for index in range(local_blocks):
                slot = z * local_blocks + index

                @pl.when(slot != me)
                def _():
                    column_copy(z, index, part, slot, me).start()

            total = total + dot2(split(product[z, part_rows(part)]), masked[at(z * cols, cols), :])
        full[part_rows(part), :] = dot3(split(total), inverse[0], inverse[1])
        for offset in range(kept):
            there = lax.rem(me // per_block + offset, window_count)
            kept_rows[me, part_rows(part), offset * block : (offset + 1) * block] = full[
                part_rows(part), at(there * block, block)
            ]
        for target in other_chips():
            row_copy(me, part, row_send.at[target, part], target * 2 + core).start()
        row_copy(me, part, row_fwd.at[chip, part], partner).start()
        place(me, part)

    column_in[me] = product[me // local_blocks, :, at(lax.rem(me, local_blocks) * block, block)]
    for step in range(1, n_row):
        source = lax.rem(me + step, n_row)
        for part in range(parts):
            column_copy(0, 0, part, source, source).wait_recv()
    for k in range(window_count):
        value = jnp.concatenate([column_in[k * per_block + index] for index in range(per_block)], axis=0)
        column_ref[k] = jnp.where(own_level <= k, -value.T, 0.0)

    for part in range(parts):
        for source in other_chips():
            forward = row_copy(source * 2 + core, part, row_fwd.at[source, part], partner)
            forward.wait_recv()
            forward.start()
            place(source * 2 + core, part)
    for part in range(parts):
        for source in [chip] + other_chips():
            row = source * 2 + 1 - core
            row_copy(row, part, row_fwd.at[source, part], partner).wait_recv()
            place(row, part)
    for lower in range(window_count):
        for offset in range(1, window_count - kept + 1):
            upper = (lower + offset) % window_count
            here = slice(offset * block, (offset + 1) * block)
            value = jnp.concatenate(
                [kept_rows[lower * per_block + index, :, here] for index in range(per_block)], axis=0
            )
            window_ref[upper * block : (upper + 1) * block, lower * block : (lower + 1) * block] = value.T

    cov_copy().wait_send()
    for group in range(2):
        for step in range(n_chip - 1):
            panel_copy(me, group, panel_send, step, partner).wait_send()
        for source in range(n_chip):
            panel_copy(me, group, panel_fwd, source, partner).wait_send()
    for part in range(parts):
        for target in other_chips():
            partial_copy(target, chip, part, target).wait_send()
        for step, target in enumerate(other_cols()):
            product_copy(col, part, step, target).wait_send()
        for step in range(1, n_row):
            column_copy(0, 0, part, lax.rem(me + step, n_row), me).wait_send()
        for target in other_chips():
            row_copy(me, part, row_send.at[target, part], target * 2 + core).wait_send()
        for source in range(n_chip):
            row_copy(me, part, row_fwd.at[source, part], partner).wait_send()


def write(column_ref, window_ref, column_hbm, window_hbm, sems):
    copies = [
        pltpu.make_async_copy(window_ref, window_hbm, sems.at[0]),
        pltpu.make_async_copy(column_ref, column_hbm, sems.at[1]),
    ]
    for copy in copies:
        copy.start()
    for copy in copies:
        copy.wait()


def solution(mesh):
    n_row, n_col = mesh.shape["prow"], mesh.shape["pcol"]

    def shards(cov_trail, factor_panel, first_level, block_slot, factor_window, diag_inverse):
        window_count, block = diag_inverse.shape[0], diag_inverse.shape[-1]
        rows, cols = cov_trail.shape
        width = window_count * block
        chunk = width // n_row
        parts = 2 if chunk % 32 == 0 else 1
        n_chip = n_row // 2
        vmem = pl.BlockSpec(memory_space=pltpu.VMEM)
        hbm = pl.BlockSpec(memory_space=pltpu.MemorySpace.HBM)
        dma = pltpu.SemaphoreType.DMA
        results = pl.pallas_call(
            functools.partial(kernel, (n_row, n_col, window_count, block, parts)),
            out_shape=(
                jax.ShapeDtypeStruct((window_count, rows, block), F32),
                jax.ShapeDtypeStruct((width, width), F32),
            ),
            in_specs=[hbm] * 6,
            out_specs=(vmem, vmem),
            scratch_shapes=[
                pltpu.SMEM(first_level.shape, jnp.int32),
                pltpu.SMEM(block_slot.shape, jnp.int32),
                pltpu.VMEM((2, rows, cols), F32),
                pltpu.VMEM((n_row,) + factor_panel.shape, BF16),
                pltpu.VMEM(factor_window.shape, BF16),
                pltpu.VMEM(diag_inverse.shape, F32),
                pltpu.VMEM((2, width, width), BF16),
                pltpu.VMEM((2, width, width), BF16),
                pltpu.VMEM((n_row * rows, width), BF16),
                pltpu.VMEM((n_chip, chunk, cols), F32),
                pltpu.VMEM((n_chip, chunk, cols), F32),
                pltpu.VMEM((n_col, chunk, cols), F32),
                pltpu.VMEM((n_row, chunk, block), F32),
                pltpu.VMEM((chunk, width), F32),
                pltpu.VMEM((n_row, chunk, (window_count // 2 + 1) * block), F32),
                dma((6,)),
                dma((1,)),
                dma((1,)),
                dma((n_chip, 2)),
                dma((n_chip, 2)),
                dma((n_row, 2)),
                dma((n_chip, parts)),
                dma((n_chip, parts)),
                dma((n_col, parts)),
                dma((n_col, parts)),
                dma((n_row, parts)),
                dma((n_row, parts)),
                dma((n_chip, parts)),
                dma((n_chip, parts)),
                dma((n_row, parts)),
            ],
            compiler_params=pltpu.CompilerParams(
                collective_id=0, has_side_effects=True, vmem_limit_bytes=40 * 1024 * 1024
            ),
        )(
            *(
                pltpu.with_memory_space_constraint(value, pltpu.MemorySpace.HBM)
                for value in (first_level, block_slot, cov_trail, factor_panel, factor_window, diag_inverse)
            )
        )
        anywhere = pl.BlockSpec(memory_space=pl.ANY)
        return pl.pallas_call(
            write,
            out_shape=tuple(jax.ShapeDtypeStruct(value.shape, F32) for value in results),
            in_specs=[anywhere] * 2,
            out_specs=(anywhere,) * 2,
            scratch_shapes=[dma((2,))],
        )(*(pltpu.with_memory_space_constraint(value, pltpu.MemorySpace.VMEM) for value in results))

    return jax.shard_map(
        shards,
        mesh=mesh,
        in_specs=(P("prow", "pcol"), P(None, "prow", None), P(), P(), P(), P()),
        out_specs=(P(None, "prow", None), P()),
        check_vma=False,
    )
```

```python
import functools

import jax
import jax.numpy as jnp
from jax import lax
from jax.experimental import pallas as pl
from jax.experimental.pallas import tpu as pltpu
from jax.sharding import PartitionSpec as P

MESH = pl.DeviceIdType.MESH
F32 = jnp.float32
BF16 = jnp.bfloat16
I16 = jnp.int16
STEPS = 32767.0
LANES = (((1,), (1,)), ((), ()))


def pair_index(upper, lower, window_count):
    return lower * window_count - lower * (lower + 1) // 2 + upper - lower - 1


def split(value):
    high = value.astype(BF16)
    return high, (value - high.astype(F32)).astype(BF16)


def dot(left, right):
    return jnp.dot(left, right, preferred_element_type=F32)


def dot2(parts, right):
    rows = parts[0].shape[0]
    both = dot(jnp.concatenate(parts, axis=0), right)
    return both[:rows] + both[rows:]


def dot3(parts, right_high, right_low):
    return dot2(parts, right_high) + dot(parts[0], right_low)


def encode(value):
    top = jnp.max(jnp.abs(value), axis=0, keepdims=True)
    some = top > 1e-33
    factor = jnp.where(some, STEPS / jnp.where(some, top, 1.0), 0.0)
    code = jnp.floor(jnp.clip(value * factor, -STEPS, STEPS) + 0.5)
    return code.astype(jnp.int32).astype(I16), top * (1.0 / STEPS)


def decode(code, scale):
    return code.astype(jnp.int32).astype(F32) * scale


def kernel(
    sizes,
    first_hbm,
    slot_hbm,
    cov_hbm,
    panel_hbm,
    factor_hbm,
    diag_hbm,
    column_ref,
    window_ref,
    first_ref,
    slot_ref,
    cov_ref,
    panels,
    factor_ref,
    diag_ref,
    inverse,
    inverse_t,
    masked,
    partial,
    partial_in,
    product,
    product_scale,
    column_in,
    column_scale,
    full,
    kept_rows,
    kept_scale,
    load_sem,
    cov_send,
    cov_recv,
    panel_send,
    panel_fwd,
    panel_recv,
    partial_send,
    partial_recv,
    product_send,
    product_recv,
    column_send,
    column_recv,
    row_send,
    row_fwd,
    row_recv,
):
    n_row, n_col, window_count, block = sizes
    n_chip = n_row // 2
    width = window_count * block
    chunk = width // n_row
    cols = cov_ref.shape[2]
    local_blocks = cols // block
    block_count = first_ref.shape[0]
    me = lax.axis_index("prow")
    col = lax.axis_index("pcol")
    core = lax.rem(me, 2)
    chip = me // 2
    partner = chip * 2 + 1 - core

    def remote(src, dst, send, recv, row, column):
        return pltpu.make_async_remote_copy(
            src_ref=src,
            dst_ref=dst,
            send_sem=send,
            recv_sem=recv,
            device_id=(row, column),
            device_id_type=MESH,
        )

    class Pair:
        def __init__(self, *copies):
            self.copies = copies

        def start(self):
            for copy in self.copies:
                copy.start()

        def wait_recv(self):
            for copy in self.copies:
                copy.wait_recv()

        def wait_send(self):
            for copy in self.copies:
                copy.wait_send()

    def pair(codes, scales, send, recv, row, column):
        return Pair(
            *(
                remote(*refs, send.at[index], recv.at[index], row, column)
                for index, refs in enumerate((codes, scales))
            )
        )

    def level_of(slot):
        level = jnp.int32(0)
        for index in range(block_count):
            level = level + jnp.where(slot_ref[index] == slot, first_ref[index], 0)
        return level

    def at(start, size):
        return pl.ds(pl.multiple_of(start, size), size)

    def other_chips():
        return [lax.rem(chip + step, n_chip) for step in range(1, n_chip)]

    def other_cols():
        return [lax.rem(col + step, n_col) for step in range(1, n_col)]

    loads = [
        pltpu.make_async_copy(source, target, load_sem.at[index])
        for index, (source, target) in enumerate(
            (
                (factor_hbm, factor_ref),
                (panel_hbm, panels.at[me]),
                (first_hbm, first_ref),
                (slot_hbm, slot_ref),
                (cov_hbm, cov_ref.at[core]),
                (diag_hbm, diag_ref),
            )
        )
    ]
    for load in loads:
        load.start()
    barrier = pltpu.get_barrier_semaphore()
    for step in range(1, n_row):
        pl.semaphore_signal(
            barrier, inc=1, device_id=(lax.rem(me + step, n_row), col), device_id_type=MESH
        )
    for step in range(1, n_col):
        pl.semaphore_signal(
            barrier, inc=1, device_id=(me, lax.rem(col + step, n_col)), device_id_type=MESH
        )

    loads[0].wait()

    def factor(w, k):
        return factor_ref[pair_index(w, k, window_count)]

    rows_id = lax.broadcasted_iota(jnp.int32, (block, block), 0)
    cols_id = lax.broadcasted_iota(jnp.int32, (block, block), 1)
    eye = jnp.where(rows_id == cols_id, 1.0, 0.0).astype(BF16)
    zero = jnp.zeros((block, block), BF16)
    inv = {}
    for distance in range(1, window_count):
        for k in range(window_count - distance):
            w = k + distance
            value = factor(w, k).astype(F32)
            for v in range(k + 1, w):
                high, low = inv[v, k]
                value = value + dot(factor(w, v), high) + dot(factor(w, v), low)
            value = -value
            inv[w, k] = split(value)
            turned = split(value.T)
            for part in range(2):
                inverse[part, w * block : (w + 1) * block, k * block : (k + 1) * block] = inv[w, k][part]
                inverse[part, k * block : (k + 1) * block, w * block : (w + 1) * block] = zero
                inverse_t[part, k * block : (k + 1) * block, w * block : (w + 1) * block] = turned[part]
                inverse_t[part, w * block : (w + 1) * block, k * block : (k + 1) * block] = zero
    for k in range(window_count):
        here = slice(k * block, (k + 1) * block)
        for target in (inverse, inverse_t):
            target[0, here, here] = eye
            target[1, here, here] = zero

    for load in loads[1:5]:
        load.wait()

    def mask(row, level):
        for k in range(window_count):
            masked[at(row * block, block), k * block : (k + 1) * block] = jnp.where(
                level <= k, panels[row, k].astype(F32), 0.0
            ).astype(BF16)

    turn = jnp.concatenate(
        [
            inverse_t[part, at((2 * target + core) * chunk, chunk), :]
            for part in range(2)
            for target in range(n_chip)
        ],
        axis=0,
    )
    half = width // 2

    def multiply(row, side):
        both = lax.dot_general(turn, masked[at(row * block, block), :], LANES, preferred_element_type=F32)
        return dot3(split(both[:half] + both[half:]), *split(cov_ref[side]))

    own_level = level_of(me)
    mask(me, own_level)
    first_half = multiply(me, core)

    pl.semaphore_wait(barrier, n_row + n_col - 2)

    def cov_copy():
        return remote(cov_ref.at[core], cov_ref.at[core], cov_send.at[0], cov_recv.at[0], partner, col)

    groups = [(0, window_count // 2), (window_count // 2, window_count)]

    def panel_copy(row, group, sems, slot, target):
        first, last = groups[group]
        here = panels.at[row, first:last]
        return remote(here, here, sems.at[slot, group], panel_recv.at[row, group], target, col)

    for group in range(2):
        panel_copy(me, group, panel_fwd, chip, partner).start()
    cov_copy().start()
    for step, target in enumerate(other_chips()):
        panel_copy(me, 0, panel_send, step, target * 2 + core).start()
    partner_level = level_of(partner)
    for group in range(2):
        panel_copy(partner, group, panel_fwd, chip, partner).wait_recv()
    mask(partner, partner_level)
    cov_copy().wait_recv()
    both_halves = first_half + multiply(partner, 1 - core)
    for target in range(n_chip):
        partial[target] = both_halves[target * chunk : (target + 1) * chunk]

    def partial_copy(source, origin, target):
        return remote(
            partial.at[source],
            partial_in.at[origin],
            partial_send.at[source],
            partial_recv.at[origin],
            target * 2 + core,
            col,
        )

    for target in other_chips():
        partial_copy(target, chip, target).start()
    for step, target in enumerate(other_chips()):
        panel_copy(me, 1, panel_send, step, target * 2 + core).start()

    def product_copy(source, step, target):
        return pair(
            (product.at[source],) * 2,
            (product_scale.at[source],) * 2,
            product_send.at[step],
            product_recv.at[source],
            me,
            target,
        )

    total = partial[chip]
    for source in other_chips():
        partial_copy(source, source, source).wait_recv()
        total = total + partial_in[source]
    product[col], product_scale[col] = encode(total)
    for step, target in enumerate(other_cols()):
        product_copy(col, step, target).start()

    loads[5].wait()
    mine = at(me * chunk, chunk)
    scaled = []
    for k in range(window_count):
        here = slice(k * block, (k + 1) * block)
        scaled.append(
            dot3((inverse_t[0, mine, here], inverse_t[1, mine, here]), *split(diag_ref[k]))
        )
    scaled = jnp.concatenate(scaled, axis=1)
    for group in range(2):
        for source in other_chips():
            forward = panel_copy(source * 2 + core, group, panel_fwd, source, partner)
            forward.wait_recv()
            forward.start()
    for source in other_chips():
        row = source * 2 + core
        mask(row, level_of(row))
    for source in other_chips():
        row = source * 2 + 1 - core
        for group in range(2):
            panel_copy(row, group, panel_fwd, source, partner).wait_recv()
        mask(row, level_of(row))

    def column_copy(z, index, target, origin):
        here = at(index * block, block)
        return pair(
            (product.at[z, :, here], column_in.at[origin]),
            (product_scale.at[z, :, here], column_scale.at[origin]),
            column_send.at[target],
            column_recv.at[origin],
            target,
            col,
        )

    kept = kept_rows.shape[2] // block
    per_block = block // chunk

    def row_copy(row, send, target):
        return pair(
            (kept_rows.at[row],) * 2, (kept_scale.at[row],) * 2, send, row_recv.at[row], target, col
        )

    def place(row):
        first = row // per_block
        for offset in range(kept):
            there = lax.rem(first + offset, window_count)
            here = slice(offset * block, (offset + 1) * block)
            window_ref[at(row * chunk, chunk), at(there * block, block)] = decode(
                kept_rows[row, :, here], kept_scale[row, :, here]
            )

    total = scaled
    for step, z in enumerate([col] + other_cols()):
        if step:
            product_copy(z, step - 1, z).wait_recv()
        for index in range(local_blocks):
            slot = z * local_blocks + index

            @pl.when(slot != me)
            def _():
                column_copy(z, index, slot, me).start()

        total = total + dot2(split(decode(product[z], product_scale[z])), masked[at(z * cols, cols), :])
    full[...] = dot3(split(total), inverse[0], inverse[1])
    for offset in range(kept):
        there = lax.rem(me // per_block + offset, window_count)
        here = slice(offset * block, (offset + 1) * block)
        kept_rows[me, :, here], kept_scale[me, :, here] = encode(full[:, at(there * block, block)])
    for target in other_chips():
        row_copy(me, row_send.at[target], target * 2 + core).start()
    row_copy(me, row_fwd.at[chip], partner).start()
    place(me)

    home = at(lax.rem(me, local_blocks) * block, block)
    column_in[me] = product[me // local_blocks, :, home]
    column_scale[me] = product_scale[me // local_blocks, :, home]
    for step in range(1, n_row):
        source = lax.rem(me + step, n_row)
        column_copy(0, 0, source, source).wait_recv()
    for k in range(window_count):
        value = jnp.concatenate(
            [
                decode(column_in[k * per_block + index], column_scale[k * per_block + index])
                for index in range(per_block)
            ],
            axis=0,
        )
        column_ref[k] = jnp.where(own_level <= k, -value.T, 0.0)

    for source in other_chips():
        forward = row_copy(source * 2 + core, row_fwd.at[source], partner)
        forward.wait_recv()
        forward.start()
        place(source * 2 + core)
    for source in [chip] + other_chips():
        row = source * 2 + 1 - core
        row_copy(row, row_fwd.at[source], partner).wait_recv()
        place(row)
    for lower in range(window_count):
        for offset in range(1, window_count - kept + 1):
            upper = (lower + offset) % window_count
            here = slice(offset * block, (offset + 1) * block)
            value = jnp.concatenate(
                [
                    decode(kept_rows[row, :, here], kept_scale[row, :, here])
                    for row in range(lower * per_block, (lower + 1) * per_block)
                ],
                axis=0,
            )
            window_ref[upper * block : (upper + 1) * block, lower * block : (lower + 1) * block] = value.T

    cov_copy().wait_send()
    for group in range(2):
        for step in range(n_chip - 1):
            panel_copy(me, group, panel_send, step, partner).wait_send()
        for source in range(n_chip):
            panel_copy(me, group, panel_fwd, source, partner).wait_send()
    for target in other_chips():
        partial_copy(target, chip, target).wait_send()
        row_copy(me, row_send.at[target], partner).wait_send()
    for step, target in enumerate(other_cols()):
        product_copy(col, step, target).wait_send()
    for step in range(1, n_row):
        column_copy(0, 0, lax.rem(me + step, n_row), me).wait_send()
    for source in range(n_chip):
        row_copy(me, row_fwd.at[source], partner).wait_send()


def write(column_ref, window_ref, column_hbm, window_hbm, sems):
    copies = [
        pltpu.make_async_copy(window_ref, window_hbm, sems.at[0]),
        pltpu.make_async_copy(column_ref, column_hbm, sems.at[1]),
    ]
    for copy in copies:
        copy.start()
    for copy in copies:
        copy.wait()


def solution(mesh):
    n_row, n_col = mesh.shape["prow"], mesh.shape["pcol"]

    def shards(cov_trail, factor_panel, first_level, block_slot, factor_window, diag_inverse):
        window_count, block = diag_inverse.shape[0], diag_inverse.shape[-1]
        rows, cols = cov_trail.shape
        width = window_count * block
        chunk = width // n_row
        n_chip = n_row // 2
        kept = (window_count // 2 + 1) * block
        vmem = pl.BlockSpec(memory_space=pltpu.VMEM)
        hbm = pl.BlockSpec(memory_space=pltpu.MemorySpace.HBM)
        dma = pltpu.SemaphoreType.DMA
        results = pl.pallas_call(
            functools.partial(kernel, (n_row, n_col, window_count, block)),
            out_shape=(
                jax.ShapeDtypeStruct((window_count, rows, block), F32),
                jax.ShapeDtypeStruct((width, width), F32),
            ),
            in_specs=[hbm] * 6,
            out_specs=(vmem, vmem),
            scratch_shapes=[
                pltpu.SMEM(first_level.shape, jnp.int32),
                pltpu.SMEM(block_slot.shape, jnp.int32),
                pltpu.VMEM((2, rows, cols), F32),
                pltpu.VMEM((n_row,) + factor_panel.shape, BF16),
                pltpu.VMEM(factor_window.shape, BF16),
                pltpu.VMEM(diag_inverse.shape, F32),
                pltpu.VMEM((2, width, width), BF16),
                pltpu.VMEM((2, width, width), BF16),
                pltpu.VMEM((n_row * rows, width), BF16),
                pltpu.VMEM((n_chip, chunk, cols), F32),
                pltpu.VMEM((n_chip, chunk, cols), F32),
                pltpu.VMEM((n_col, chunk, cols), I16),
                pltpu.VMEM((n_col, 1, cols), F32),
                pltpu.VMEM((n_row, chunk, block), I16),
                pltpu.VMEM((n_row, 1, block), F32),
                pltpu.VMEM((chunk, width), F32),
                pltpu.VMEM((n_row, chunk, kept), I16),
                pltpu.VMEM((n_row, 1, kept), F32),
                dma((6,)),
                dma((1,)),
                dma((1,)),
                dma((n_chip, 2)),
                dma((n_chip, 2)),
                dma((n_row, 2)),
                dma((n_chip,)),
                dma((n_chip,)),
                dma((n_col, 2)),
                dma((n_col, 2)),
                dma((n_row, 2)),
                dma((n_row, 2)),
                dma((n_chip, 2)),
                dma((n_chip, 2)),
                dma((n_row, 2)),
            ],
            compiler_params=pltpu.CompilerParams(
                collective_id=0, has_side_effects=True, vmem_limit_bytes=40 * 1024 * 1024
            ),
        )(
            *(
                pltpu.with_memory_space_constraint(value, pltpu.MemorySpace.HBM)
                for value in (first_level, block_slot, cov_trail, factor_panel, factor_window, diag_inverse)
            )
        )
        anywhere = pl.BlockSpec(memory_space=pl.ANY)
        return pl.pallas_call(
            write,
            out_shape=tuple(jax.ShapeDtypeStruct(value.shape, F32) for value in results),
            in_specs=[anywhere] * 2,
            out_specs=(anywhere,) * 2,
            scratch_shapes=[dma((2,))],
        )(*(pltpu.with_memory_space_constraint(value, pltpu.MemorySpace.VMEM) for value in results))

    return jax.shard_map(
        shards,
        mesh=mesh,
        in_specs=(P("prow", "pcol"), P(None, "prow", None), P(), P(), P(), P()),
        out_specs=(P(None, "prow", None), P()),
        check_vma=False,
    )
```

```python
import functools

import jax
import jax.numpy as jnp
from jax import lax
from jax.experimental import pallas as pl
from jax.experimental.pallas import tpu as pltpu
from jax.sharding import PartitionSpec as P

MESH = pl.DeviceIdType.MESH
F32 = jnp.float32
BF16 = jnp.bfloat16
I16 = jnp.int16
STEPS = 32767.0
LANES = (((1,), (1,)), ((), ()))


def pair_index(upper, lower, window_count):
    return lower * window_count - lower * (lower + 1) // 2 + upper - lower - 1


def split(value):
    high = value.astype(BF16)
    return high, (value - high.astype(F32)).astype(BF16)


def dot(left, right):
    return jnp.dot(left, right, preferred_element_type=F32)


def dot2(parts, right):
    rows = parts[0].shape[0]
    both = dot(jnp.concatenate(parts, axis=0), right)
    return both[:rows] + both[rows:]


def dot3(parts, right_high, right_low):
    return dot2(parts, right_high) + dot(parts[0], right_low)


def encode(value):
    top = jnp.max(jnp.abs(value), axis=0, keepdims=True)
    some = top > 1e-33
    factor = jnp.where(some, STEPS / jnp.where(some, top, 1.0), 0.0)
    code = jnp.floor(jnp.clip(value * factor, -STEPS, STEPS) + 0.5)
    return code.astype(jnp.int32).astype(I16), top * (1.0 / STEPS)


def decode(code, scale):
    return code.astype(jnp.int32).astype(F32) * scale


def kernel(
    sizes,
    first_hbm,
    slot_hbm,
    cov_hbm,
    panel_hbm,
    factor_hbm,
    diag_hbm,
    column_ref,
    window_ref,
    first_ref,
    slot_ref,
    cov_ref,
    panels,
    factor_ref,
    diag_ref,
    inverse,
    inverse_t,
    masked,
    partial,
    partial_scale,
    partial_in,
    partial_in_scale,
    product,
    product_scale,
    column_in,
    column_scale,
    full,
    kept_rows,
    kept_scale,
    load_sem,
    cov_send,
    cov_recv,
    panel_send,
    panel_fwd,
    panel_recv,
    partial_send,
    partial_recv,
    product_send,
    product_recv,
    column_send,
    column_recv,
    row_send,
    row_fwd,
    row_recv,
):
    n_row, n_col, window_count, block = sizes
    n_chip = n_row // 2
    width = window_count * block
    chunk = width // n_row
    cols = cov_ref.shape[2]
    local_blocks = cols // block
    block_count = first_ref.shape[0]
    me = lax.axis_index("prow")
    col = lax.axis_index("pcol")
    core = lax.rem(me, 2)
    chip = me // 2
    partner = chip * 2 + 1 - core

    def remote(src, dst, send, recv, row, column):
        return pltpu.make_async_remote_copy(
            src_ref=src,
            dst_ref=dst,
            send_sem=send,
            recv_sem=recv,
            device_id=(row, column),
            device_id_type=MESH,
        )

    class Pair:
        def __init__(self, *copies):
            self.copies = copies

        def start(self):
            for copy in self.copies:
                copy.start()

        def wait_recv(self):
            for copy in self.copies:
                copy.wait_recv()

        def wait_send(self):
            for copy in self.copies:
                copy.wait_send()

    def pair(codes, scales, send, recv, row, column):
        return Pair(
            *(
                remote(*refs, send.at[index], recv.at[index], row, column)
                for index, refs in enumerate((codes, scales))
            )
        )

    def level_of(slot):
        level = jnp.int32(0)
        for index in range(block_count):
            level = level + jnp.where(slot_ref[index] == slot, first_ref[index], 0)
        return level

    def at(start, size):
        return pl.ds(pl.multiple_of(start, size), size)

    def other_chips():
        return [lax.rem(chip + step, n_chip) for step in range(1, n_chip)]

    def other_cols():
        return [lax.rem(col + step, n_col) for step in range(1, n_col)]

    loads = [
        pltpu.make_async_copy(source, target, load_sem.at[index])
        for index, (source, target) in enumerate(
            (
                (factor_hbm, factor_ref),
                (panel_hbm, panels.at[me]),
                (first_hbm, first_ref),
                (slot_hbm, slot_ref),
                (cov_hbm, cov_ref.at[core]),
                (diag_hbm, diag_ref),
            )
        )
    ]
    for load in loads:
        load.start()
    barrier = pltpu.get_barrier_semaphore()
    for step in range(1, n_row):
        pl.semaphore_signal(
            barrier, inc=1, device_id=(lax.rem(me + step, n_row), col), device_id_type=MESH
        )
    for step in range(1, n_col):
        pl.semaphore_signal(
            barrier, inc=1, device_id=(me, lax.rem(col + step, n_col)), device_id_type=MESH
        )

    loads[0].wait()

    def factor(w, k):
        return factor_ref[pair_index(w, k, window_count)]

    rows_id = lax.broadcasted_iota(jnp.int32, (block, block), 0)
    cols_id = lax.broadcasted_iota(jnp.int32, (block, block), 1)
    eye = jnp.where(rows_id == cols_id, 1.0, 0.0).astype(BF16)
    zero = jnp.zeros((block, block), BF16)
    inv = {}
    for distance in range(1, window_count):
        for k in range(window_count - distance):
            w = k + distance
            value = factor(w, k).astype(F32)
            for v in range(k + 1, w):
                high, low = inv[v, k]
                value = value + dot(factor(w, v), high) + dot(factor(w, v), low)
            value = -value
            inv[w, k] = split(value)
            turned = split(value.T)
            for part in range(2):
                inverse[part, w * block : (w + 1) * block, k * block : (k + 1) * block] = inv[w, k][part]
                inverse[part, k * block : (k + 1) * block, w * block : (w + 1) * block] = zero
                inverse_t[part, k * block : (k + 1) * block, w * block : (w + 1) * block] = turned[part]
                inverse_t[part, w * block : (w + 1) * block, k * block : (k + 1) * block] = zero
    for k in range(window_count):
        here = slice(k * block, (k + 1) * block)
        for target in (inverse, inverse_t):
            target[0, here, here] = eye
            target[1, here, here] = zero

    for load in loads[1:5]:
        load.wait()

    pl.semaphore_wait(barrier, n_row + n_col - 2)

    def cov_copy():
        return remote(cov_ref.at[core], cov_ref.at[core], cov_send.at[0], cov_recv.at[0], partner, col)

    groups = [(0, window_count // 2), (window_count // 2, window_count)]

    def panel_copy(row, group, sems, slot, target):
        first, last = groups[group]
        here = panels.at[row, first:last]
        return remote(here, here, sems.at[slot, group], panel_recv.at[row, group], target, col)

    for group in range(2):
        panel_copy(me, group, panel_fwd, chip, partner).start()
    cov_copy().start()
    for step, target in enumerate(other_chips()):
        panel_copy(me, 0, panel_send, step, target * 2 + core).start()
    def mask(row, level):
        for k in range(window_count):
            masked[at(row * block, block), k * block : (k + 1) * block] = jnp.where(
                level <= k, panels[row, k].astype(F32), 0.0
            ).astype(BF16)

    turn = jnp.concatenate(
        [
            inverse_t[part, at((2 * target + core) * chunk, chunk), :]
            for part in range(2)
            for target in range(n_chip)
        ],
        axis=0,
    )
    half = width // 2

    def multiply(row, side):
        both = lax.dot_general(turn, masked[at(row * block, block), :], LANES, preferred_element_type=F32)
        return dot3(split(both[:half] + both[half:]), *split(cov_ref[side]))

    own_level = level_of(me)
    mask(me, own_level)
    first_half = multiply(me, core)

    partner_level = level_of(partner)
    for group in range(2):
        panel_copy(partner, group, panel_fwd, chip, partner).wait_recv()
    mask(partner, partner_level)
    cov_copy().wait_recv()
    both_halves = first_half + multiply(partner, 1 - core)
    for target in range(n_chip):
        partial[target], partial_scale[target] = encode(both_halves[target * chunk : (target + 1) * chunk])

    def partial_copy(source, origin, target):
        return pair(
            (partial.at[source], partial_in.at[origin]),
            (partial_scale.at[source], partial_in_scale.at[origin]),
            partial_send.at[source],
            partial_recv.at[origin],
            target * 2 + core,
            col,
        )

    for target in other_chips():
        partial_copy(target, chip, target).start()
    for step, target in enumerate(other_chips()):
        panel_copy(me, 1, panel_send, step, target * 2 + core).start()

    def product_copy(source, step, target):
        return pair(
            (product.at[source],) * 2,
            (product_scale.at[source],) * 2,
            product_send.at[step],
            product_recv.at[source],
            me,
            target,
        )

    total = decode(partial[chip], partial_scale[chip])
    for source in other_chips():
        partial_copy(source, source, source).wait_recv()
        total = total + decode(partial_in[source], partial_in_scale[source])
    product[col], product_scale[col] = encode(total)
    for step, target in enumerate(other_cols()):
        product_copy(col, step, target).start()

    loads[5].wait()
    mine = at(me * chunk, chunk)
    scaled = []
    for k in range(window_count):
        here = slice(k * block, (k + 1) * block)
        scaled.append(
            dot3((inverse_t[0, mine, here], inverse_t[1, mine, here]), *split(diag_ref[k]))
        )
    scaled = jnp.concatenate(scaled, axis=1)
    for group in range(2):
        for source in other_chips():
            forward = panel_copy(source * 2 + core, group, panel_fwd, source, partner)
            forward.wait_recv()
            forward.start()
    for source in other_chips():
        row = source * 2 + core
        mask(row, level_of(row))
    for source in other_chips():
        row = source * 2 + 1 - core
        for group in range(2):
            panel_copy(row, group, panel_fwd, source, partner).wait_recv()
        mask(row, level_of(row))

    def column_copy(z, index, target, origin):
        here = at(index * block, block)
        return pair(
            (product.at[z, :, here], column_in.at[origin]),
            (product_scale.at[z, :, here], column_scale.at[origin]),
            column_send.at[target],
            column_recv.at[origin],
            target,
            col,
        )

    kept = kept_rows.shape[2] // block
    per_block = block // chunk

    def row_copy(row, send, target):
        return pair(
            (kept_rows.at[row],) * 2, (kept_scale.at[row],) * 2, send, row_recv.at[row], target, col
        )

    def place(row):
        first = row // per_block
        for offset in range(kept):
            there = lax.rem(first + offset, window_count)
            here = slice(offset * block, (offset + 1) * block)
            window_ref[at(row * chunk, chunk), at(there * block, block)] = decode(
                kept_rows[row, :, here], kept_scale[row, :, here]
            )

    total = scaled
    for step, z in enumerate([col] + other_cols()):
        if step:
            product_copy(z, step - 1, z).wait_recv()
        for index in range(local_blocks):
            slot = z * local_blocks + index

            @pl.when(slot != me)
            def _():
                column_copy(z, index, slot, me).start()

        total = total + dot2(split(decode(product[z], product_scale[z])), masked[at(z * cols, cols), :])
    full[...] = dot3(split(total), inverse[0], inverse[1])
    for offset in range(kept):
        there = lax.rem(me // per_block + offset, window_count)
        here = slice(offset * block, (offset + 1) * block)
        kept_rows[me, :, here], kept_scale[me, :, here] = encode(full[:, at(there * block, block)])
    for target in other_chips():
        row_copy(me, row_send.at[target], target * 2 + core).start()
    row_copy(me, row_fwd.at[chip], partner).start()
    place(me)

    home = at(lax.rem(me, local_blocks) * block, block)
    column_in[me] = product[me // local_blocks, :, home]
    column_scale[me] = product_scale[me // local_blocks, :, home]
    for step in range(1, n_row):
        source = lax.rem(me + step, n_row)
        column_copy(0, 0, source, source).wait_recv()
    for k in range(window_count):
        value = jnp.concatenate(
            [
                decode(column_in[k * per_block + index], column_scale[k * per_block + index])
                for index in range(per_block)
            ],
            axis=0,
        )
        column_ref[k] = jnp.where(own_level <= k, -value.T, 0.0)

    for source in other_chips():
        forward = row_copy(source * 2 + core, row_fwd.at[source], partner)
        forward.wait_recv()
        forward.start()
        place(source * 2 + core)
    for source in [chip] + other_chips():
        row = source * 2 + 1 - core
        row_copy(row, row_fwd.at[source], partner).wait_recv()
        place(row)
    for lower in range(window_count):
        for offset in range(1, window_count - kept + 1):
            upper = (lower + offset) % window_count
            here = slice(offset * block, (offset + 1) * block)
            value = jnp.concatenate(
                [
                    decode(kept_rows[row, :, here], kept_scale[row, :, here])
                    for row in range(lower * per_block, (lower + 1) * per_block)
                ],
                axis=0,
            )
            window_ref[upper * block : (upper + 1) * block, lower * block : (lower + 1) * block] = value.T

    cov_copy().wait_send()
    for group in range(2):
        for step in range(n_chip - 1):
            panel_copy(me, group, panel_send, step, partner).wait_send()
        for source in range(n_chip):
            panel_copy(me, group, panel_fwd, source, partner).wait_send()
    for target in other_chips():
        partial_copy(target, chip, target).wait_send()
        row_copy(me, row_send.at[target], partner).wait_send()
    for step, target in enumerate(other_cols()):
        product_copy(col, step, target).wait_send()
    for step in range(1, n_row):
        column_copy(0, 0, lax.rem(me + step, n_row), me).wait_send()
    for source in range(n_chip):
        row_copy(me, row_fwd.at[source], partner).wait_send()


def write(column_ref, window_ref, column_hbm, window_hbm, sems):
    copies = [
        pltpu.make_async_copy(window_ref, window_hbm, sems.at[0]),
        pltpu.make_async_copy(column_ref, column_hbm, sems.at[1]),
    ]
    for copy in copies:
        copy.start()
    for copy in copies:
        copy.wait()


def solution(mesh):
    n_row, n_col = mesh.shape["prow"], mesh.shape["pcol"]

    def shards(cov_trail, factor_panel, first_level, block_slot, factor_window, diag_inverse):
        window_count, block = diag_inverse.shape[0], diag_inverse.shape[-1]
        rows, cols = cov_trail.shape
        width = window_count * block
        chunk = width // n_row
        n_chip = n_row // 2
        kept = (window_count // 2 + 1) * block
        vmem = pl.BlockSpec(memory_space=pltpu.VMEM)
        hbm = pl.BlockSpec(memory_space=pltpu.MemorySpace.HBM)
        dma = pltpu.SemaphoreType.DMA
        results = pl.pallas_call(
            functools.partial(kernel, (n_row, n_col, window_count, block)),
            out_shape=(
                jax.ShapeDtypeStruct((window_count, rows, block), F32),
                jax.ShapeDtypeStruct((width, width), F32),
            ),
            in_specs=[hbm] * 6,
            out_specs=(vmem, vmem),
            scratch_shapes=[
                pltpu.SMEM(first_level.shape, jnp.int32),
                pltpu.SMEM(block_slot.shape, jnp.int32),
                pltpu.VMEM((2, rows, cols), F32),
                pltpu.VMEM((n_row,) + factor_panel.shape, BF16),
                pltpu.VMEM(factor_window.shape, BF16),
                pltpu.VMEM(diag_inverse.shape, F32),
                pltpu.VMEM((2, width, width), BF16),
                pltpu.VMEM((2, width, width), BF16),
                pltpu.VMEM((n_row * rows, width), BF16),
                pltpu.VMEM((n_chip, chunk, cols), I16),
                pltpu.VMEM((n_chip, 1, cols), F32),
                pltpu.VMEM((n_chip, chunk, cols), I16),
                pltpu.VMEM((n_chip, 1, cols), F32),
                pltpu.VMEM((n_col, chunk, cols), I16),
                pltpu.VMEM((n_col, 1, cols), F32),
                pltpu.VMEM((n_row, chunk, block), I16),
                pltpu.VMEM((n_row, 1, block), F32),
                pltpu.VMEM((chunk, width), F32),
                pltpu.VMEM((n_row, chunk, kept), I16),
                pltpu.VMEM((n_row, 1, kept), F32),
                dma((6,)),
                dma((1,)),
                dma((1,)),
                dma((n_chip, 2)),
                dma((n_chip, 2)),
                dma((n_row, 2)),
                dma((n_chip, 2)),
                dma((n_chip, 2)),
                dma((n_col, 2)),
                dma((n_col, 2)),
                dma((n_row, 2)),
                dma((n_row, 2)),
                dma((n_chip, 2)),
                dma((n_chip, 2)),
                dma((n_row, 2)),
            ],
            compiler_params=pltpu.CompilerParams(
                collective_id=0, has_side_effects=True, vmem_limit_bytes=40 * 1024 * 1024
            ),
        )(
            *(
                pltpu.with_memory_space_constraint(value, pltpu.MemorySpace.HBM)
                for value in (first_level, block_slot, cov_trail, factor_panel, factor_window, diag_inverse)
            )
        )
        anywhere = pl.BlockSpec(memory_space=pl.ANY)
        return pl.pallas_call(
            write,
            out_shape=tuple(jax.ShapeDtypeStruct(value.shape, F32) for value in results),
            in_specs=[anywhere] * 2,
            out_specs=(anywhere,) * 2,
            scratch_shapes=[dma((2,))],
        )(*(pltpu.with_memory_space_constraint(value, pltpu.MemorySpace.VMEM) for value in results))

    return jax.shard_map(
        shards,
        mesh=mesh,
        in_specs=(P("prow", "pcol"), P(None, "prow", None), P(), P(), P(), P()),
        out_specs=(P(None, "prow", None), P()),
        check_vma=False,
    )
```

```python
import functools

import jax
import jax.numpy as jnp
from jax import lax
from jax.experimental import pallas as pl
from jax.experimental.pallas import tpu as pltpu
from jax.sharding import PartitionSpec as P

MESH = pl.DeviceIdType.MESH
F32 = jnp.float32
BF16 = jnp.bfloat16
I16 = jnp.int16
STEPS = 32767.0
LANES = (((1,), (1,)), ((), ()))


def pair_index(upper, lower, window_count):
    return lower * window_count - lower * (lower + 1) // 2 + upper - lower - 1


def split(value):
    high = value.astype(BF16)
    return high, (value - high.astype(F32)).astype(BF16)


def dot(left, right):
    return jnp.dot(left, right, preferred_element_type=F32)


def dot2(parts, right):
    rows = parts[0].shape[0]
    both = dot(jnp.concatenate(parts, axis=0), right)
    return both[:rows] + both[rows:]


def dot3(parts, right_high, right_low):
    return dot2(parts, right_high) + dot(parts[0], right_low)


def encode(value):
    top = jnp.max(jnp.abs(value), axis=0, keepdims=True)
    some = top > 1e-33
    factor = jnp.where(some, STEPS / jnp.where(some, top, 1.0), 0.0)
    code = jnp.floor(jnp.clip(value * factor, -STEPS, STEPS) + 0.5)
    return code.astype(jnp.int32).astype(I16), top * (1.0 / STEPS)


def decode(code, scale):
    return code.astype(jnp.int32).astype(F32) * scale


def kernel(
    sizes,
    first_hbm,
    slot_hbm,
    cov_hbm,
    panel_hbm,
    factor_hbm,
    diag_hbm,
    column_ref,
    window_ref,
    first_ref,
    slot_ref,
    cov_ref,
    panels,
    factor_ref,
    diag_ref,
    inverse,
    inverse_t,
    masked,
    partial,
    partial_scale,
    partial_in,
    partial_in_scale,
    product,
    product_scale,
    column_in,
    column_scale,
    full,
    kept_rows,
    kept_scale,
    load_sem,
    cov_send,
    cov_recv,
    panel_send,
    panel_fwd,
    panel_recv,
    partial_send,
    partial_recv,
    product_send,
    product_recv,
    column_send,
    column_recv,
    row_send,
    row_fwd,
    row_recv,
):
    n_row, n_col, window_count, block = sizes
    n_chip = n_row // 2
    width = window_count * block
    chunk = width // n_row
    cols = cov_ref.shape[2]
    local_blocks = cols // block
    block_count = first_ref.shape[0]
    me = lax.axis_index("prow")
    col = lax.axis_index("pcol")
    core = lax.rem(me, 2)
    chip = me // 2
    partner = chip * 2 + 1 - core

    def remote(src, dst, send, recv, row, column):
        return pltpu.make_async_remote_copy(
            src_ref=src,
            dst_ref=dst,
            send_sem=send,
            recv_sem=recv,
            device_id=(row, column),
            device_id_type=MESH,
        )

    class Pair:
        def __init__(self, *copies):
            self.copies = copies

        def start(self):
            for copy in self.copies:
                copy.start()

        def wait_recv(self):
            for copy in self.copies:
                copy.wait_recv()

        def wait_send(self):
            for copy in self.copies:
                copy.wait_send()

    def pair(codes, scales, send, recv, row, column):
        return Pair(
            *(
                remote(*refs, send.at[index], recv.at[index], row, column)
                for index, refs in enumerate((codes, scales))
            )
        )

    def level_of(slot):
        level = jnp.int32(0)
        for index in range(block_count):
            level = level + jnp.where(slot_ref[index] == slot, first_ref[index], 0)
        return level

    def at(start, size):
        return pl.ds(pl.multiple_of(start, size), size)

    def other_chips():
        return [lax.rem(chip + step, n_chip) for step in range(1, n_chip)]

    def other_cols():
        return [lax.rem(col + step, n_col) for step in range(1, n_col)]

    loads = [
        pltpu.make_async_copy(source, target, load_sem.at[index])
        for index, (source, target) in enumerate(
            (
                (panel_hbm, panels.at[me]),
                (cov_hbm, cov_ref.at[core]),
                (factor_hbm, factor_ref),
                (first_hbm, first_ref),
                (slot_hbm, slot_ref),
                (diag_hbm, diag_ref),
            )
        )
    ]
    for load in loads:
        load.start()
    barrier = pltpu.get_barrier_semaphore()
    for step in range(1, n_row):
        pl.semaphore_signal(
            barrier, inc=1, device_id=(lax.rem(me + step, n_row), col), device_id_type=MESH
        )
    for step in range(1, n_col):
        pl.semaphore_signal(
            barrier, inc=1, device_id=(me, lax.rem(col + step, n_col)), device_id_type=MESH
        )

    for load in loads[:2]:
        load.wait()

    pl.semaphore_wait(barrier, n_row + n_col - 2)

    def cov_copy():
        return remote(cov_ref.at[core], cov_ref.at[core], cov_send.at[0], cov_recv.at[0], partner, col)

    groups = [(0, window_count // 2), (window_count // 2, window_count)]

    def panel_copy(row, group, sems, slot, target):
        first, last = groups[group]
        here = panels.at[row, first:last]
        return remote(here, here, sems.at[slot, group], panel_recv.at[row, group], target, col)

    for group in range(2):
        panel_copy(me, group, panel_fwd, chip, partner).start()
    cov_copy().start()
    for step, target in enumerate(other_chips()):
        panel_copy(me, 0, panel_send, step, target * 2 + core).start()

    for load in loads[2:5]:
        load.wait()

    def factor(w, k):
        return factor_ref[pair_index(w, k, window_count)]

    rows_id = lax.broadcasted_iota(jnp.int32, (block, block), 0)
    cols_id = lax.broadcasted_iota(jnp.int32, (block, block), 1)
    eye = jnp.where(rows_id == cols_id, 1.0, 0.0).astype(BF16)
    zero = jnp.zeros((block, block), BF16)
    inv = {}
    for distance in range(1, window_count):
        for k in range(window_count - distance):
            w = k + distance
            value = factor(w, k).astype(F32)
            for v in range(k + 1, w):
                high, low = inv[v, k]
                value = value + dot(factor(w, v), high) + dot(factor(w, v), low)
            value = -value
            inv[w, k] = split(value)
            turned = split(value.T)
            for part in range(2):
                inverse[part, w * block : (w + 1) * block, k * block : (k + 1) * block] = inv[w, k][part]
                inverse[part, k * block : (k + 1) * block, w * block : (w + 1) * block] = zero
                inverse_t[part, k * block : (k + 1) * block, w * block : (w + 1) * block] = turned[part]
                inverse_t[part, w * block : (w + 1) * block, k * block : (k + 1) * block] = zero
    for k in range(window_count):
        here = slice(k * block, (k + 1) * block)
        for target in (inverse, inverse_t):
            target[0, here, here] = eye
            target[1, here, here] = zero

    def mask(row, level):
        for k in range(window_count):
            masked[at(row * block, block), k * block : (k + 1) * block] = jnp.where(
                level <= k, panels[row, k].astype(F32), 0.0
            ).astype(BF16)

    turn = jnp.concatenate(
        [
            inverse_t[part, at((2 * target + core) * chunk, chunk), :]
            for part in range(2)
            for target in range(n_chip)
        ],
        axis=0,
    )
    half = width // 2

    def multiply(row, side):
        both = lax.dot_general(turn, masked[at(row * block, block), :], LANES, preferred_element_type=F32)
        return dot3(split(both[:half] + both[half:]), *split(cov_ref[side]))

    own_level = level_of(me)
    mask(me, own_level)
    first_half = multiply(me, core)

    partner_level = level_of(partner)
    for group in range(2):
        panel_copy(partner, group, panel_fwd, chip, partner).wait_recv()
    mask(partner, partner_level)
    cov_copy().wait_recv()
    both_halves = first_half + multiply(partner, 1 - core)
    for target in range(n_chip):
        partial[target], partial_scale[target] = encode(both_halves[target * chunk : (target + 1) * chunk])

    def partial_copy(source, origin, target):
        return pair(
            (partial.at[source], partial_in.at[origin]),
            (partial_scale.at[source], partial_in_scale.at[origin]),
            partial_send.at[source],
            partial_recv.at[origin],
            target * 2 + core,
            col,
        )

    for target in other_chips():
        partial_copy(target, chip, target).start()
    for step, target in enumerate(other_chips()):
        partial_copy(target, chip, target).wait_send()
        panel_copy(me, 1, panel_send, step, target * 2 + core).start()

    def product_copy(source, step, target):
        return pair(
            (product.at[source],) * 2,
            (product_scale.at[source],) * 2,
            product_send.at[step],
            product_recv.at[source],
            me,
            target,
        )

    def column_copy(z, index, target, origin):
        here = at(index * block, block)
        return pair(
            (product.at[z, :, here], column_in.at[origin]),
            (product_scale.at[z, :, here], column_scale.at[origin]),
            column_send.at[target],
            column_recv.at[origin],
            target,
            col,
        )

    def send_columns(z):
        for index in range(local_blocks):
            slot = z * local_blocks + index

            @pl.when(slot != me)
            def _():
                column_copy(z, index, slot, me).start()

    total = decode(partial[chip], partial_scale[chip])
    for source in other_chips():
        partial_copy(source, source, source).wait_recv()
        total = total + decode(partial_in[source], partial_in_scale[source])
    product[col], product_scale[col] = encode(total)
    for step, target in enumerate(other_cols()):
        product_copy(col, step, target).start()
    send_columns(col)

    loads[5].wait()
    mine = at(me * chunk, chunk)
    scaled = []
    for k in range(window_count):
        here = slice(k * block, (k + 1) * block)
        scaled.append(
            dot3((inverse_t[0, mine, here], inverse_t[1, mine, here]), *split(diag_ref[k]))
        )
    scaled = jnp.concatenate(scaled, axis=1)
    for group in range(2):
        for source in other_chips():
            forward = panel_copy(source * 2 + core, group, panel_fwd, source, partner)
            forward.wait_recv()
            forward.start()
    for source in other_chips():
        row = source * 2 + core
        mask(row, level_of(row))
    for source in other_chips():
        row = source * 2 + 1 - core
        for group in range(2):
            panel_copy(row, group, panel_fwd, source, partner).wait_recv()
        mask(row, level_of(row))

    kept = kept_rows.shape[2] // block
    per_block = block // chunk

    def row_copy(row, send, target):
        return pair(
            (kept_rows.at[row],) * 2, (kept_scale.at[row],) * 2, send, row_recv.at[row], target, col
        )

    def place(row):
        first = row // per_block
        for offset in range(kept):
            there = lax.rem(first + offset, window_count)
            here = slice(offset * block, (offset + 1) * block)
            window_ref[at(row * chunk, chunk), at(there * block, block)] = decode(
                kept_rows[row, :, here], kept_scale[row, :, here]
            )

    total = scaled
    for step, z in enumerate([col] + other_cols()):
        if step:
            product_copy(z, step - 1, z).wait_recv()
        if 0 < step < n_col - 1:
            send_columns(z)
        total = total + dot2(split(decode(product[z], product_scale[z])), masked[at(z * cols, cols), :])
    full[...] = dot3(split(total), inverse[0], inverse[1])
    for offset in range(kept):
        there = lax.rem(me // per_block + offset, window_count)
        here = slice(offset * block, (offset + 1) * block)
        kept_rows[me, :, here], kept_scale[me, :, here] = encode(full[:, at(there * block, block)])
    for target in other_chips():
        row_copy(me, row_send.at[target], target * 2 + core).start()
    row_copy(me, row_fwd.at[chip], partner).start()
    send_columns(lax.rem(col + n_col - 1, n_col))
    place(me)

    home = at(lax.rem(me, local_blocks) * block, block)
    column_in[me] = product[me // local_blocks, :, home]
    column_scale[me] = product_scale[me // local_blocks, :, home]
    for step in range(1, n_row):
        source = lax.rem(me + step, n_row)
        column_copy(0, 0, source, source).wait_recv()
    for k in range(window_count):
        value = jnp.concatenate(
            [
                decode(column_in[k * per_block + index], column_scale[k * per_block + index])
                for index in range(per_block)
            ],
            axis=0,
        )
        column_ref[k] = jnp.where(own_level <= k, -value.T, 0.0)

    cov_copy().wait_send()
    for group in range(2):
        for step in range(n_chip - 1):
            panel_copy(me, group, panel_send, step, partner).wait_send()
        for source in range(n_chip):
            panel_copy(me, group, panel_fwd, source, partner).wait_send()
    for step, target in enumerate(other_cols()):
        product_copy(col, step, target).wait_send()
    for step in range(1, n_row):
        column_copy(0, 0, lax.rem(me + step, n_row), me).wait_send()

    for source in other_chips():
        forward = row_copy(source * 2 + core, row_fwd.at[source], partner)
        forward.wait_recv()
        forward.start()
        place(source * 2 + core)
    for source in [chip] + other_chips():
        row = source * 2 + 1 - core
        row_copy(row, row_fwd.at[source], partner).wait_recv()
        place(row)
    for lower in range(window_count):
        for offset in range(1, window_count - kept + 1):
            upper = (lower + offset) % window_count
            here = slice(offset * block, (offset + 1) * block)
            value = jnp.concatenate(
                [
                    decode(kept_rows[row, :, here], kept_scale[row, :, here])
                    for row in range(lower * per_block, (lower + 1) * per_block)
                ],
                axis=0,
            )
            window_ref[upper * block : (upper + 1) * block, lower * block : (lower + 1) * block] = value.T

    for target in other_chips():
        row_copy(me, row_send.at[target], partner).wait_send()
    for source in range(n_chip):
        row_copy(me, row_fwd.at[source], partner).wait_send()


def write(column_ref, window_ref, column_hbm, window_hbm, sems):
    copies = [
        pltpu.make_async_copy(window_ref, window_hbm, sems.at[0]),
        pltpu.make_async_copy(column_ref, column_hbm, sems.at[1]),
    ]
    for copy in copies:
        copy.start()
    for copy in copies:
        copy.wait()


def solution(mesh):
    n_row, n_col = mesh.shape["prow"], mesh.shape["pcol"]

    def shards(cov_trail, factor_panel, first_level, block_slot, factor_window, diag_inverse):
        window_count, block = diag_inverse.shape[0], diag_inverse.shape[-1]
        rows, cols = cov_trail.shape
        width = window_count * block
        chunk = width // n_row
        n_chip = n_row // 2
        kept = (window_count // 2 + 1) * block
        vmem = pl.BlockSpec(memory_space=pltpu.VMEM)
        hbm = pl.BlockSpec(memory_space=pltpu.MemorySpace.HBM)
        dma = pltpu.SemaphoreType.DMA
        results = pl.pallas_call(
            functools.partial(kernel, (n_row, n_col, window_count, block)),
            out_shape=(
                jax.ShapeDtypeStruct((window_count, rows, block), F32),
                jax.ShapeDtypeStruct((width, width), F32),
            ),
            in_specs=[hbm] * 6,
            out_specs=(vmem, vmem),
            scratch_shapes=[
                pltpu.SMEM(first_level.shape, jnp.int32),
                pltpu.SMEM(block_slot.shape, jnp.int32),
                pltpu.VMEM((2, rows, cols), F32),
                pltpu.VMEM((n_row,) + factor_panel.shape, BF16),
                pltpu.VMEM(factor_window.shape, BF16),
                pltpu.VMEM(diag_inverse.shape, F32),
                pltpu.VMEM((2, width, width), BF16),
                pltpu.VMEM((2, width, width), BF16),
                pltpu.VMEM((n_row * rows, width), BF16),
                pltpu.VMEM((n_chip, chunk, cols), I16),
                pltpu.VMEM((n_chip, 1, cols), F32),
                pltpu.VMEM((n_chip, chunk, cols), I16),
                pltpu.VMEM((n_chip, 1, cols), F32),
                pltpu.VMEM((n_col, chunk, cols), I16),
                pltpu.VMEM((n_col, 1, cols), F32),
                pltpu.VMEM((n_row, chunk, block), I16),
                pltpu.VMEM((n_row, 1, block), F32),
                pltpu.VMEM((chunk, width), F32),
                pltpu.VMEM((n_row, chunk, kept), I16),
                pltpu.VMEM((n_row, 1, kept), F32),
                dma((6,)),
                dma((1,)),
                dma((1,)),
                dma((n_chip, 2)),
                dma((n_chip, 2)),
                dma((n_row, 2)),
                dma((n_chip, 2)),
                dma((n_chip, 2)),
                dma((n_col, 2)),
                dma((n_col, 2)),
                dma((n_row, 2)),
                dma((n_row, 2)),
                dma((n_chip, 2)),
                dma((n_chip, 2)),
                dma((n_row, 2)),
            ],
            compiler_params=pltpu.CompilerParams(
                collective_id=0, has_side_effects=True, vmem_limit_bytes=40 * 1024 * 1024
            ),
        )(
            *(
                pltpu.with_memory_space_constraint(value, pltpu.MemorySpace.HBM)
                for value in (first_level, block_slot, cov_trail, factor_panel, factor_window, diag_inverse)
            )
        )
        anywhere = pl.BlockSpec(memory_space=pl.ANY)
        return pl.pallas_call(
            write,
            out_shape=tuple(jax.ShapeDtypeStruct(value.shape, F32) for value in results),
            in_specs=[anywhere] * 2,
            out_specs=(anywhere,) * 2,
            scratch_shapes=[dma((2,))],
        )(*(pltpu.with_memory_space_constraint(value, pltpu.MemorySpace.VMEM) for value in results))

    return jax.shard_map(
        shards,
        mesh=mesh,
        in_specs=(P("prow", "pcol"), P(None, "prow", None), P(), P(), P(), P()),
        out_specs=(P(None, "prow", None), P()),
        check_vma=False,
    )
```

```python
import functools

import jax
import jax.numpy as jnp
from jax import lax
from jax.experimental import pallas as pl
from jax.experimental.pallas import tpu as pltpu
from jax.sharding import PartitionSpec as P

MESH = pl.DeviceIdType.MESH
F32 = jnp.float32
BF16 = jnp.bfloat16
I16 = jnp.int16
STEPS = 32767.0
LANES = (((1,), (1,)), ((), ()))


def pair_index(upper, lower, window_count):
    return lower * window_count - lower * (lower + 1) // 2 + upper - lower - 1


def split(value):
    high = value.astype(BF16)
    return high, (value - high.astype(F32)).astype(BF16)


def dot(left, right):
    return jnp.dot(left, right, preferred_element_type=F32)


def dot2(parts, right):
    rows = parts[0].shape[0]
    both = dot(jnp.concatenate(parts, axis=0), right)
    return both[:rows] + both[rows:]


def dot3(parts, right_high, right_low):
    return dot2(parts, right_high) + dot(parts[0], right_low)


def encode(value):
    top = jnp.max(jnp.abs(value), axis=0, keepdims=True)
    some = top > 1e-33
    factor = jnp.where(some, STEPS / jnp.where(some, top, 1.0), 0.0)
    code = jnp.floor(jnp.clip(value * factor, -STEPS, STEPS) + 0.5)
    return code.astype(jnp.int32).astype(I16), top * (1.0 / STEPS)


def decode(code, scale):
    return code.astype(jnp.int32).astype(F32) * scale


def kernel(
    sizes,
    first_hbm,
    slot_hbm,
    cov_hbm,
    panel_hbm,
    factor_hbm,
    diag_hbm,
    column_ref,
    window_ref,
    first_ref,
    slot_ref,
    cov_ref,
    panels,
    factor_ref,
    diag_ref,
    inverse,
    inverse_t,
    masked,
    partial,
    partial_scale,
    partial_in,
    partial_in_scale,
    product,
    product_scale,
    column_in,
    column_scale,
    full,
    kept_rows,
    kept_scale,
    load_sem,
    cov_send,
    cov_recv,
    panel_send,
    panel_fwd,
    panel_recv,
    partial_send,
    partial_recv,
    product_send,
    product_recv,
    column_send,
    column_recv,
    row_send,
    row_fwd,
    row_recv,
):
    n_row, n_col, window_count, block = sizes
    n_chip = n_row // 2
    width = window_count * block
    chunk = width // n_row
    cols = cov_ref.shape[2]
    local_blocks = cols // block
    block_count = first_ref.shape[0]
    me = lax.axis_index("prow")
    col = lax.axis_index("pcol")
    core = lax.rem(me, 2)
    chip = me // 2
    partner = chip * 2 + 1 - core

    def remote(src, dst, send, recv, row, column):
        return pltpu.make_async_remote_copy(
            src_ref=src,
            dst_ref=dst,
            send_sem=send,
            recv_sem=recv,
            device_id=(row, column),
            device_id_type=MESH,
        )

    class Pair:
        def __init__(self, *copies):
            self.copies = copies

        def start(self):
            for copy in self.copies:
                copy.start()

        def wait_recv(self):
            for copy in self.copies:
                copy.wait_recv()

        def wait_send(self):
            for copy in self.copies:
                copy.wait_send()

    def pair(codes, scales, send, recv, row, column):
        return Pair(
            *(
                remote(*refs, send.at[index], recv.at[index], row, column)
                for index, refs in enumerate((codes, scales))
            )
        )

    def level_of(slot):
        level = jnp.int32(0)
        for index in range(block_count):
            level = level + jnp.where(slot_ref[index] == slot, first_ref[index], 0)
        return level

    def at(start, size):
        return pl.ds(pl.multiple_of(start, size), size)

    def other_chips():
        return [lax.rem(chip + step, n_chip) for step in range(1, n_chip)]

    def other_cols():
        return [lax.rem(col + step, n_col) for step in range(1, n_col)]

    loads = [
        pltpu.make_async_copy(source, target, load_sem.at[index])
        for index, (source, target) in enumerate(
            (
                (panel_hbm, panels.at[me]),
                (cov_hbm, cov_ref.at[core]),
                (factor_hbm, factor_ref),
                (first_hbm, first_ref),
                (slot_hbm, slot_ref),
                (diag_hbm, diag_ref),
            )
        )
    ]
    for load in loads:
        load.start()
    barrier = pltpu.get_barrier_semaphore()
    for step in range(1, n_row):
        pl.semaphore_signal(
            barrier, inc=1, device_id=(lax.rem(me + step, n_row), col), device_id_type=MESH
        )
    for step in range(1, n_col):
        pl.semaphore_signal(
            barrier, inc=1, device_id=(me, lax.rem(col + step, n_col)), device_id_type=MESH
        )

    for load in loads[:2]:
        load.wait()

    pl.semaphore_wait(barrier, n_row + n_col - 2)

    def cov_copy():
        return remote(cov_ref.at[core], cov_ref.at[core], cov_send.at[0], cov_recv.at[0], partner, col)

    groups = [(0, window_count // 2), (window_count // 2, window_count)]

    def panel_copy(row, group, sems, slot, target):
        first, last = groups[group]
        here = panels.at[row, first:last]
        return remote(here, here, sems.at[slot, group], panel_recv.at[row, group], target, col)

    for group in range(2):
        panel_copy(me, group, panel_fwd, chip, partner).start()
    cov_copy().start()
    square = n_chip == 4
    near = (chip + 1 - 2 * lax.rem(chip, 2), lax.rem(chip + 2, n_chip))
    far = lax.rem(near[0] + 2, n_chip)
    for group in range(2):
        for step, target in enumerate(near if square else other_chips()):
            panel_copy(me, group, panel_send, step, target * 2 + core).start()

    for load in loads[2:5]:
        load.wait()

    def factor(w, k):
        return factor_ref[pair_index(w, k, window_count)]

    rows_id = lax.broadcasted_iota(jnp.int32, (block, block), 0)
    cols_id = lax.broadcasted_iota(jnp.int32, (block, block), 1)
    eye = jnp.where(rows_id == cols_id, 1.0, 0.0).astype(BF16)
    zero = jnp.zeros((block, block), BF16)
    inv = {}
    for distance in range(1, window_count):
        for k in range(window_count - distance):
            w = k + distance
            value = factor(w, k).astype(F32)
            for v in range(k + 1, w):
                high, low = inv[v, k]
                value = value + dot(factor(w, v), high) + dot(factor(w, v), low)
            value = -value
            inv[w, k] = split(value)
            turned = split(value.T)
            for part in range(2):
                inverse[part, w * block : (w + 1) * block, k * block : (k + 1) * block] = inv[w, k][part]
                inverse[part, k * block : (k + 1) * block, w * block : (w + 1) * block] = zero
                inverse_t[part, k * block : (k + 1) * block, w * block : (w + 1) * block] = turned[part]
                inverse_t[part, w * block : (w + 1) * block, k * block : (k + 1) * block] = zero
    for k in range(window_count):
        here = slice(k * block, (k + 1) * block)
        for target in (inverse, inverse_t):
            target[0, here, here] = eye
            target[1, here, here] = zero

    def mask(row, level):
        for k in range(window_count):
            masked[at(row * block, block), k * block : (k + 1) * block] = jnp.where(
                level <= k, panels[row, k].astype(F32), 0.0
            ).astype(BF16)

    turn = jnp.concatenate(
        [
            inverse_t[part, at((2 * target + core) * chunk, chunk), :]
            for part in range(2)
            for target in range(n_chip)
        ],
        axis=0,
    )
    half = width // 2

    def multiply(row, side):
        both = lax.dot_general(turn, masked[at(row * block, block), :], LANES, preferred_element_type=F32)
        return dot3(split(both[:half] + both[half:]), *split(cov_ref[side]))

    own_level = level_of(me)
    mask(me, own_level)
    first_half = multiply(me, core)

    partner_level = level_of(partner)
    for group in range(2):
        panel_copy(partner, group, panel_fwd, chip, partner).wait_recv()
    mask(partner, partner_level)
    cov_copy().wait_recv()
    both_halves = first_half + multiply(partner, 1 - core)
    for target in range(n_chip):
        partial[target], partial_scale[target] = encode(both_halves[target * chunk : (target + 1) * chunk])

    def partial_copy(source, origin, target):
        return pair(
            (partial.at[source], partial_in.at[origin]),
            (partial_scale.at[source], partial_in_scale.at[origin]),
            partial_send.at[source],
            partial_recv.at[origin],
            target * 2 + core,
            col,
        )

    for target in other_chips():
        partial_copy(target, chip, target).start()

    def relay(group):
        row = near[group] * 2 + core
        return panel_copy(row, group, panel_send, n_chip - 2, near[1 - group] * 2 + core)

    if square:
        for group in range(2):
            relay(group).wait_recv()
            relay(group).start()

    def product_copy(source, step, target):
        return pair(
            (product.at[source],) * 2,
            (product_scale.at[source],) * 2,
            product_send.at[step],
            product_recv.at[source],
            me,
            target,
        )

    def column_copy(z, index, target, origin):
        here = at(index * block, block)
        return pair(
            (product.at[z, :, here], column_in.at[origin]),
            (product_scale.at[z, :, here], column_scale.at[origin]),
            column_send.at[target],
            column_recv.at[origin],
            target,
            col,
        )

    def send_columns(z):
        for index in range(local_blocks):
            slot = z * local_blocks + index

            @pl.when(slot != me)
            def _():
                column_copy(z, index, slot, me).start()

    total = decode(partial[chip], partial_scale[chip])
    for source in other_chips():
        partial_copy(source, source, source).wait_recv()
        total = total + decode(partial_in[source], partial_in_scale[source])
    product[col], product_scale[col] = encode(total)
    for step, target in enumerate(other_cols()):
        product_copy(col, step, target).start()
    send_columns(col)

    loads[5].wait()
    mine = at(me * chunk, chunk)
    scaled = []
    for k in range(window_count):
        here = slice(k * block, (k + 1) * block)
        scaled.append(
            dot3((inverse_t[0, mine, here], inverse_t[1, mine, here]), *split(diag_ref[k]))
        )
    scaled = jnp.concatenate(scaled, axis=1)
    def pass_on(source, group, fresh=True):
        forward = panel_copy(source * 2 + core, group, panel_fwd, source, partner)
        if fresh:
            forward.wait_recv()
        forward.start()

    if square:
        pass_on(near[0], 0, False)
        pass_on(near[1], 1, False)
        for source, group in ((near[0], 1), (near[1], 0), (far, 0), (far, 1)):
            pass_on(source, group)
    else:
        for group in range(2):
            for source in other_chips():
                pass_on(source, group)
    for source in other_chips():
        row = source * 2 + core
        mask(row, level_of(row))
    for source in other_chips():
        row = source * 2 + 1 - core
        for group in range(2):
            panel_copy(row, group, panel_fwd, source, partner).wait_recv()
        mask(row, level_of(row))

    kept = kept_rows.shape[2] // block
    per_block = block // chunk

    def row_copy(row, send, target):
        return pair(
            (kept_rows.at[row],) * 2, (kept_scale.at[row],) * 2, send, row_recv.at[row], target, col
        )

    def place(row):
        first = row // per_block
        for offset in range(kept):
            there = lax.rem(first + offset, window_count)
            here = slice(offset * block, (offset + 1) * block)
            window_ref[at(row * chunk, chunk), at(there * block, block)] = decode(
                kept_rows[row, :, here], kept_scale[row, :, here]
            )

    total = scaled
    for step, z in enumerate([col] + other_cols()):
        if step:
            product_copy(z, step - 1, z).wait_recv()
        if 0 < step < n_col - 1:
            send_columns(z)
        total = total + dot2(split(decode(product[z], product_scale[z])), masked[at(z * cols, cols), :])
    full[...] = dot3(split(total), inverse[0], inverse[1])
    for offset in range(kept):
        there = lax.rem(me // per_block + offset, window_count)
        here = slice(offset * block, (offset + 1) * block)
        kept_rows[me, :, here], kept_scale[me, :, here] = encode(full[:, at(there * block, block)])
    for target in other_chips():
        row_copy(me, row_send.at[target], target * 2 + core).start()
    row_copy(me, row_fwd.at[chip], partner).start()
    send_columns(lax.rem(col + n_col - 1, n_col))
    place(me)

    for target in other_chips():
        partial_copy(target, chip, target).wait_send()
    cov_copy().wait_send()
    for group in range(2):
        for step in range(n_chip - 1):
            panel_copy(me, group, panel_send, step, partner).wait_send()
        for source in range(n_chip):
            panel_copy(me, group, panel_fwd, source, partner).wait_send()
    for step, target in enumerate(other_cols()):
        product_copy(col, step, target).wait_send()
    for step in range(1, n_row):
        column_copy(0, 0, lax.rem(me + step, n_row), me).wait_send()

    for source in other_chips():
        forward = row_copy(source * 2 + core, row_fwd.at[source], partner)
        forward.wait_recv()
        forward.start()
        place(source * 2 + core)
    home = at(lax.rem(me, local_blocks) * block, block)
    column_in[me] = product[me // local_blocks, :, home]
    column_scale[me] = product_scale[me // local_blocks, :, home]
    for step in range(1, n_row):
        source = lax.rem(me + step, n_row)
        column_copy(0, 0, source, source).wait_recv()
    for k in range(window_count):
        value = jnp.concatenate(
            [
                decode(column_in[k * per_block + index], column_scale[k * per_block + index])
                for index in range(per_block)
            ],
            axis=0,
        )
        column_ref[k] = jnp.where(own_level <= k, -value.T, 0.0)

    for source in [chip] + other_chips():
        row = source * 2 + 1 - core
        row_copy(row, row_fwd.at[source], partner).wait_recv()
        place(row)
    for lower in range(window_count):
        for offset in range(1, window_count - kept + 1):
            upper = (lower + offset) % window_count
            here = slice(offset * block, (offset + 1) * block)
            value = jnp.concatenate(
                [
                    decode(kept_rows[row, :, here], kept_scale[row, :, here])
                    for row in range(lower * per_block, (lower + 1) * per_block)
                ],
                axis=0,
            )
            window_ref[upper * block : (upper + 1) * block, lower * block : (lower + 1) * block] = value.T

    for target in other_chips():
        row_copy(me, row_send.at[target], partner).wait_send()
    for source in range(n_chip):
        row_copy(me, row_fwd.at[source], partner).wait_send()


def write(column_ref, window_ref, column_hbm, window_hbm, sems):
    copies = [
        pltpu.make_async_copy(window_ref, window_hbm, sems.at[0]),
        pltpu.make_async_copy(column_ref, column_hbm, sems.at[1]),
    ]
    for copy in copies:
        copy.start()
    for copy in copies:
        copy.wait()


def solution(mesh):
    n_row, n_col = mesh.shape["prow"], mesh.shape["pcol"]

    def shards(cov_trail, factor_panel, first_level, block_slot, factor_window, diag_inverse):
        window_count, block = diag_inverse.shape[0], diag_inverse.shape[-1]
        rows, cols = cov_trail.shape
        width = window_count * block
        chunk = width // n_row
        n_chip = n_row // 2
        kept = (window_count // 2 + 1) * block
        vmem = pl.BlockSpec(memory_space=pltpu.VMEM)
        hbm = pl.BlockSpec(memory_space=pltpu.MemorySpace.HBM)
        dma = pltpu.SemaphoreType.DMA
        results = pl.pallas_call(
            functools.partial(kernel, (n_row, n_col, window_count, block)),
            out_shape=(
                jax.ShapeDtypeStruct((window_count, rows, block), F32),
                jax.ShapeDtypeStruct((width, width), F32),
            ),
            in_specs=[hbm] * 6,
            out_specs=(vmem, vmem),
            scratch_shapes=[
                pltpu.SMEM(first_level.shape, jnp.int32),
                pltpu.SMEM(block_slot.shape, jnp.int32),
                pltpu.VMEM((2, rows, cols), F32),
                pltpu.VMEM((n_row,) + factor_panel.shape, BF16),
                pltpu.VMEM(factor_window.shape, BF16),
                pltpu.VMEM(diag_inverse.shape, F32),
                pltpu.VMEM((2, width, width), BF16),
                pltpu.VMEM((2, width, width), BF16),
                pltpu.VMEM((n_row * rows, width), BF16),
                pltpu.VMEM((n_chip, chunk, cols), I16),
                pltpu.VMEM((n_chip, 1, cols), F32),
                pltpu.VMEM((n_chip, chunk, cols), I16),
                pltpu.VMEM((n_chip, 1, cols), F32),
                pltpu.VMEM((n_col, chunk, cols), I16),
                pltpu.VMEM((n_col, 1, cols), F32),
                pltpu.VMEM((n_row, chunk, block), I16),
                pltpu.VMEM((n_row, 1, block), F32),
                pltpu.VMEM((chunk, width), F32),
                pltpu.VMEM((n_row, chunk, kept), I16),
                pltpu.VMEM((n_row, 1, kept), F32),
                dma((6,)),
                dma((1,)),
                dma((1,)),
                dma((n_chip, 2)),
                dma((n_chip, 2)),
                dma((n_row, 2)),
                dma((n_chip, 2)),
                dma((n_chip, 2)),
                dma((n_col, 2)),
                dma((n_col, 2)),
                dma((n_row, 2)),
                dma((n_row, 2)),
                dma((n_chip, 2)),
                dma((n_chip, 2)),
                dma((n_row, 2)),
            ],
            compiler_params=pltpu.CompilerParams(
                collective_id=0, has_side_effects=True, vmem_limit_bytes=40 * 1024 * 1024
            ),
        )(
            *(
                pltpu.with_memory_space_constraint(value, pltpu.MemorySpace.HBM)
                for value in (first_level, block_slot, cov_trail, factor_panel, factor_window, diag_inverse)
            )
        )
        anywhere = pl.BlockSpec(memory_space=pl.ANY)
        return pl.pallas_call(
            write,
            out_shape=tuple(jax.ShapeDtypeStruct(value.shape, F32) for value in results),
            in_specs=[anywhere] * 2,
            out_specs=(anywhere,) * 2,
            scratch_shapes=[dma((2,))],
        )(*(pltpu.with_memory_space_constraint(value, pltpu.MemorySpace.VMEM) for value in results))

    return jax.shard_map(
        shards,
        mesh=mesh,
        in_specs=(P("prow", "pcol"), P(None, "prow", None), P(), P(), P(), P()),
        out_specs=(P(None, "prow", None), P()),
        check_vma=False,
    )
```

```python
import functools

import jax
import jax.numpy as jnp
from jax import lax
from jax.experimental import pallas as pl
from jax.experimental.pallas import tpu as pltpu
from jax.sharding import PartitionSpec as P

MESH = pl.DeviceIdType.MESH
F32 = jnp.float32
BF16 = jnp.bfloat16
I16 = jnp.int16
STEPS = 32767.0
LANES = (((1,), (1,)), ((), ()))


def pair_index(upper, lower, window_count):
    return lower * window_count - lower * (lower + 1) // 2 + upper - lower - 1


def split(value):
    high = value.astype(BF16)
    return high, (value - high.astype(F32)).astype(BF16)


def dot(left, right):
    return jnp.dot(left, right, preferred_element_type=F32)


def dot2(parts, right):
    rows = parts[0].shape[0]
    both = dot(jnp.concatenate(parts, axis=0), right)
    return both[:rows] + both[rows:]


def dot3(parts, right_high, right_low):
    return dot2(parts, right_high) + dot(parts[0], right_low)


def encode(value):
    top = jnp.max(jnp.abs(value), axis=0, keepdims=True)
    some = top > 1e-33
    factor = jnp.where(some, STEPS / jnp.where(some, top, 1.0), 0.0)
    code = jnp.floor(jnp.clip(value * factor, -STEPS, STEPS) + 0.5)
    return code.astype(jnp.int32).astype(I16), top * (1.0 / STEPS)


def decode(code, scale):
    return code.astype(jnp.int32).astype(F32) * scale


def kernel(
    sizes,
    first_hbm,
    slot_hbm,
    cov_hbm,
    panel_hbm,
    factor_hbm,
    diag_hbm,
    column_ref,
    window_ref,
    first_ref,
    slot_ref,
    cov_ref,
    panels,
    factor_ref,
    diag_ref,
    inverse,
    inverse_t,
    masked,
    partial,
    partial_scale,
    partial_in,
    partial_in_scale,
    product,
    product_scale,
    column_in,
    column_scale,
    full,
    kept_rows,
    kept_scale,
    load_sem,
    cov_send,
    cov_recv,
    panel_send,
    panel_fwd,
    panel_recv,
    partial_send,
    partial_recv,
    product_send,
    product_recv,
    column_send,
    column_recv,
    row_send,
    row_fwd,
    row_recv,
):
    n_row, n_col, window_count, block = sizes
    n_chip = n_row // 2
    width = window_count * block
    chunk = width // n_row
    cols = cov_ref.shape[2]
    local_blocks = cols // block
    block_count = first_ref.shape[0]
    me = lax.axis_index("prow")
    col = lax.axis_index("pcol")
    core = lax.rem(me, 2)
    chip = me // 2
    partner = chip * 2 + 1 - core

    def remote(src, dst, send, recv, row, column):
        return pltpu.make_async_remote_copy(
            src_ref=src,
            dst_ref=dst,
            send_sem=send,
            recv_sem=recv,
            device_id=(row, column),
            device_id_type=MESH,
        )

    class Pair:
        def __init__(self, *copies):
            self.copies = copies

        def start(self):
            for copy in self.copies:
                copy.start()

        def wait_recv(self):
            for copy in self.copies:
                copy.wait_recv()

        def wait_send(self):
            for copy in self.copies:
                copy.wait_send()

    def pair(codes, scales, send, recv, row, column):
        return Pair(
            *(
                remote(*refs, send.at[index], recv.at[index], row, column)
                for index, refs in enumerate((codes, scales))
            )
        )

    def level_of(slot):
        level = jnp.int32(0)
        for index in range(block_count):
            level = level + jnp.where(slot_ref[index] == slot, first_ref[index], 0)
        return level

    def at(start, size):
        return pl.ds(pl.multiple_of(start, size), size)

    def other_chips():
        if n_chip == 4:
            side = chip + 1 - 2 * lax.rem(chip, 2)
            return [lax.rem(side + 2, 4), side, lax.rem(chip + 2, 4)]
        return [lax.rem(chip + step, n_chip) for step in range(1, n_chip)]

    def other_cols():
        return [lax.rem(col + step, n_col) for step in range(1, n_col)]

    loads = [
        pltpu.make_async_copy(source, target, load_sem.at[index])
        for index, (source, target) in enumerate(
            (
                (panel_hbm, panels.at[me]),
                (cov_hbm, cov_ref.at[core]),
                (factor_hbm, factor_ref),
                (first_hbm, first_ref),
                (slot_hbm, slot_ref),
                (diag_hbm, diag_ref),
            )
        )
    ]
    for load in loads:
        load.start()
    barrier = pltpu.get_barrier_semaphore()
    for step in range(1, n_row):
        pl.semaphore_signal(
            barrier, inc=1, device_id=(lax.rem(me + step, n_row), col), device_id_type=MESH
        )
    for step in range(1, n_col):
        pl.semaphore_signal(
            barrier, inc=1, device_id=(me, lax.rem(col + step, n_col)), device_id_type=MESH
        )

    for load in loads[:2]:
        load.wait()

    pl.semaphore_wait(barrier, n_row + n_col - 2)

    def cov_copy():
        return remote(cov_ref.at[core], cov_ref.at[core], cov_send.at[0], cov_recv.at[0], partner, col)

    groups = [(0, window_count // 2), (window_count // 2, window_count)]

    def panel_copy(row, group, sems, slot, target):
        first, last = groups[group]
        here = panels.at[row, first:last]
        return remote(here, here, sems.at[slot, group], panel_recv.at[row, group], target, col)

    for group in range(2):
        panel_copy(me, group, panel_fwd, chip, partner).start()
    cov_copy().start()
    square = n_chip == 4
    near = (chip + 1 - 2 * lax.rem(chip, 2), lax.rem(chip + 2, n_chip))
    far = lax.rem(near[0] + 2, n_chip)
    for group in range(2):
        for step, target in enumerate(near if square else other_chips()):
            panel_copy(me, group, panel_send, step, target * 2 + core).start()

    for load in loads[2:5]:
        load.wait()

    def factor(w, k):
        return factor_ref[pair_index(w, k, window_count)]

    rows_id = lax.broadcasted_iota(jnp.int32, (block, block), 0)
    cols_id = lax.broadcasted_iota(jnp.int32, (block, block), 1)
    eye = jnp.where(rows_id == cols_id, 1.0, 0.0).astype(BF16)
    zero = jnp.zeros((block, block), BF16)
    inv = {}
    for distance in range(1, window_count):
        for k in range(window_count - distance):
            w = k + distance
            value = factor(w, k).astype(F32)
            for v in range(k + 1, w):
                high, low = inv[v, k]
                value = value + dot(factor(w, v), high) + dot(factor(w, v), low)
            value = -value
            inv[w, k] = split(value)
            turned = split(value.T)
            for part in range(2):
                inverse[part, w * block : (w + 1) * block, k * block : (k + 1) * block] = inv[w, k][part]
                inverse[part, k * block : (k + 1) * block, w * block : (w + 1) * block] = zero
                inverse_t[part, k * block : (k + 1) * block, w * block : (w + 1) * block] = turned[part]
                inverse_t[part, w * block : (w + 1) * block, k * block : (k + 1) * block] = zero
    for k in range(window_count):
        here = slice(k * block, (k + 1) * block)
        for target in (inverse, inverse_t):
            target[0, here, here] = eye
            target[1, here, here] = zero

    def mask(row, level):
        for k in range(window_count):
            masked[at(row * block, block), k * block : (k + 1) * block] = jnp.where(
                level <= k, panels[row, k].astype(F32), 0.0
            ).astype(BF16)

    turn = jnp.concatenate(
        [
            inverse_t[part, at((2 * target + core) * chunk, chunk), :]
            for part in range(2)
            for target in range(n_chip)
        ],
        axis=0,
    )
    half = width // 2

    def multiply(row, side):
        both = lax.dot_general(turn, masked[at(row * block, block), :], LANES, preferred_element_type=F32)
        return dot3(split(both[:half] + both[half:]), *split(cov_ref[side]))

    own_level = level_of(me)
    mask(me, own_level)
    first_half = multiply(me, core)

    partner_level = level_of(partner)
    for group in range(2):
        panel_copy(partner, group, panel_fwd, chip, partner).wait_recv()
    mask(partner, partner_level)
    cov_copy().wait_recv()
    both_halves = first_half + multiply(partner, 1 - core)
    for target in range(n_chip):
        partial[target], partial_scale[target] = encode(both_halves[target * chunk : (target + 1) * chunk])

    def partial_copy(source, origin, target):
        return pair(
            (partial.at[source], partial_in.at[origin]),
            (partial_scale.at[source], partial_in_scale.at[origin]),
            partial_send.at[source],
            partial_recv.at[origin],
            target * 2 + core,
            col,
        )

    for target in other_chips():
        partial_copy(target, chip, target).start()

    def relay(group):
        row = near[group] * 2 + core
        return panel_copy(row, group, panel_send, n_chip - 2, near[1 - group] * 2 + core)

    if square:
        for group in range(2):
            relay(group).wait_recv()
            relay(group).start()

    def product_copy(source, step, target):
        return pair(
            (product.at[source],) * 2,
            (product_scale.at[source],) * 2,
            product_send.at[step],
            product_recv.at[source],
            me,
            target,
        )

    def column_copy(z, index, target, origin):
        here = at(index * block, block)
        return pair(
            (product.at[z, :, here], column_in.at[origin]),
            (product_scale.at[z, :, here], column_scale.at[origin]),
            column_send.at[target],
            column_recv.at[origin],
            target,
            col,
        )

    def send_columns(z):
        for index in range(local_blocks):
            slot = z * local_blocks + index

            @pl.when(slot != me)
            def _():
                column_copy(z, index, slot, me).start()

    total = decode(partial[chip], partial_scale[chip])
    for source in other_chips():
        partial_copy(source, source, source).wait_recv()
        total = total + decode(partial_in[source], partial_in_scale[source])
    product[col], product_scale[col] = encode(total)
    for step, target in enumerate(other_cols()):
        product_copy(col, step, target).start()
    send_columns(col)

    loads[5].wait()
    mine = at(me * chunk, chunk)
    scaled = []
    for k in range(window_count):
        here = slice(k * block, (k + 1) * block)
        scaled.append(
            dot3((inverse_t[0, mine, here], inverse_t[1, mine, here]), *split(diag_ref[k]))
        )
    scaled = jnp.concatenate(scaled, axis=1)
    def pass_on(source, group, fresh=True):
        forward = panel_copy(source * 2 + core, group, panel_fwd, source, partner)
        if fresh:
            forward.wait_recv()
        forward.start()

    if square:
        pass_on(near[0], 0, False)
        pass_on(near[1], 1, False)
        for source, group in ((near[0], 1), (near[1], 0), (far, 0), (far, 1)):
            pass_on(source, group)
    else:
        for group in range(2):
            for source in other_chips():
                pass_on(source, group)
    for source in other_chips():
        row = source * 2 + core
        mask(row, level_of(row))
    for source in other_chips():
        row = source * 2 + 1 - core
        for group in range(2):
            panel_copy(row, group, panel_fwd, source, partner).wait_recv()
        mask(row, level_of(row))

    kept = kept_rows.shape[2] // block
    per_block = block // chunk

    def row_copy(row, send, target):
        return pair(
            (kept_rows.at[row],) * 2, (kept_scale.at[row],) * 2, send, row_recv.at[row], target, col
        )

    def place(row):
        first = row // per_block
        for offset in range(kept):
            there = lax.rem(first + offset, window_count)
            here = slice(offset * block, (offset + 1) * block)
            window_ref[at(row * chunk, chunk), at(there * block, block)] = decode(
                kept_rows[row, :, here], kept_scale[row, :, here]
            )

    total = scaled
    for step, z in enumerate([col] + other_cols()):
        if step:
            product_copy(z, step - 1, z).wait_recv()
        if 0 < step < n_col - 1:
            send_columns(z)
        total = total + dot2(split(decode(product[z], product_scale[z])), masked[at(z * cols, cols), :])
    full[...] = dot3(split(total), inverse[0], inverse[1])
    for offset in range(kept):
        there = lax.rem(me // per_block + offset, window_count)
        here = slice(offset * block, (offset + 1) * block)
        kept_rows[me, :, here], kept_scale[me, :, here] = encode(full[:, at(there * block, block)])
    for target in other_chips():
        row_copy(me, row_send.at[target], target * 2 + core).start()
    row_copy(me, row_fwd.at[chip], partner).start()
    send_columns(lax.rem(col + n_col - 1, n_col))
    place(me)

    for target in other_chips():
        partial_copy(target, chip, target).wait_send()
    cov_copy().wait_send()
    for group in range(2):
        for step in range(n_chip - 1):
            panel_copy(me, group, panel_send, step, partner).wait_send()
        for source in range(n_chip):
            panel_copy(me, group, panel_fwd, source, partner).wait_send()
    for step, target in enumerate(other_cols()):
        product_copy(col, step, target).wait_send()
    for step in range(1, n_row):
        column_copy(0, 0, lax.rem(me + step, n_row), me).wait_send()

    for source in other_chips():
        forward = row_copy(source * 2 + core, row_fwd.at[source], partner)
        forward.wait_recv()
        forward.start()
        place(source * 2 + core)
    home = at(lax.rem(me, local_blocks) * block, block)
    column_in[me] = product[me // local_blocks, :, home]
    column_scale[me] = product_scale[me // local_blocks, :, home]
    for step in range(1, n_row):
        source = lax.rem(me + step, n_row)
        column_copy(0, 0, source, source).wait_recv()
    for k in range(window_count):
        value = jnp.concatenate(
            [
                decode(column_in[k * per_block + index], column_scale[k * per_block + index])
                for index in range(per_block)
            ],
            axis=0,
        )
        column_ref[k] = jnp.where(own_level <= k, -value.T, 0.0)

    for source in [chip] + other_chips():
        row = source * 2 + 1 - core
        row_copy(row, row_fwd.at[source], partner).wait_recv()
        place(row)
    for lower in range(window_count):
        for offset in range(1, window_count - kept + 1):
            upper = (lower + offset) % window_count
            here = slice(offset * block, (offset + 1) * block)
            value = jnp.concatenate(
                [
                    decode(kept_rows[row, :, here], kept_scale[row, :, here])
                    for row in range(lower * per_block, (lower + 1) * per_block)
                ],
                axis=0,
            )
            window_ref[upper * block : (upper + 1) * block, lower * block : (lower + 1) * block] = value.T

    for target in other_chips():
        row_copy(me, row_send.at[target], partner).wait_send()
    for source in range(n_chip):
        row_copy(me, row_fwd.at[source], partner).wait_send()


def write(column_ref, window_ref, column_hbm, window_hbm, sems):
    copies = [
        pltpu.make_async_copy(window_ref, window_hbm, sems.at[0]),
        pltpu.make_async_copy(column_ref, column_hbm, sems.at[1]),
    ]
    for copy in copies:
        copy.start()
    for copy in copies:
        copy.wait()


def solution(mesh):
    n_row, n_col = mesh.shape["prow"], mesh.shape["pcol"]

    def shards(cov_trail, factor_panel, first_level, block_slot, factor_window, diag_inverse):
        window_count, block = diag_inverse.shape[0], diag_inverse.shape[-1]
        rows, cols = cov_trail.shape
        width = window_count * block
        chunk = width // n_row
        n_chip = n_row // 2
        kept = (window_count // 2 + 1) * block
        vmem = pl.BlockSpec(memory_space=pltpu.VMEM)
        hbm = pl.BlockSpec(memory_space=pltpu.MemorySpace.HBM)
        dma = pltpu.SemaphoreType.DMA
        results = pl.pallas_call(
            functools.partial(kernel, (n_row, n_col, window_count, block)),
            out_shape=(
                jax.ShapeDtypeStruct((window_count, rows, block), F32),
                jax.ShapeDtypeStruct((width, width), F32),
            ),
            in_specs=[hbm] * 6,
            out_specs=(vmem, vmem),
            scratch_shapes=[
                pltpu.SMEM(first_level.shape, jnp.int32),
                pltpu.SMEM(block_slot.shape, jnp.int32),
                pltpu.VMEM((2, rows, cols), F32),
                pltpu.VMEM((n_row,) + factor_panel.shape, BF16),
                pltpu.VMEM(factor_window.shape, BF16),
                pltpu.VMEM(diag_inverse.shape, F32),
                pltpu.VMEM((2, width, width), BF16),
                pltpu.VMEM((2, width, width), BF16),
                pltpu.VMEM((n_row * rows, width), BF16),
                pltpu.VMEM((n_chip, chunk, cols), I16),
                pltpu.VMEM((n_chip, 1, cols), F32),
                pltpu.VMEM((n_chip, chunk, cols), I16),
                pltpu.VMEM((n_chip, 1, cols), F32),
                pltpu.VMEM((n_col, chunk, cols), I16),
                pltpu.VMEM((n_col, 1, cols), F32),
                pltpu.VMEM((n_row, chunk, block), I16),
                pltpu.VMEM((n_row, 1, block), F32),
                pltpu.VMEM((chunk, width), F32),
                pltpu.VMEM((n_row, chunk, kept), I16),
                pltpu.VMEM((n_row, 1, kept), F32),
                dma((6,)),
                dma((1,)),
                dma((1,)),
                dma((n_chip, 2)),
                dma((n_chip, 2)),
                dma((n_row, 2)),
                dma((n_chip, 2)),
                dma((n_chip, 2)),
                dma((n_col, 2)),
                dma((n_col, 2)),
                dma((n_row, 2)),
                dma((n_row, 2)),
                dma((n_chip, 2)),
                dma((n_chip, 2)),
                dma((n_row, 2)),
            ],
            compiler_params=pltpu.CompilerParams(
                collective_id=0, has_side_effects=True, vmem_limit_bytes=40 * 1024 * 1024
            ),
        )(
            *(
                pltpu.with_memory_space_constraint(value, pltpu.MemorySpace.HBM)
                for value in (first_level, block_slot, cov_trail, factor_panel, factor_window, diag_inverse)
            )
        )
        anywhere = pl.BlockSpec(memory_space=pl.ANY)
        return pl.pallas_call(
            write,
            out_shape=tuple(jax.ShapeDtypeStruct(value.shape, F32) for value in results),
            in_specs=[anywhere] * 2,
            out_specs=(anywhere,) * 2,
            scratch_shapes=[dma((2,))],
        )(*(pltpu.with_memory_space_constraint(value, pltpu.MemorySpace.VMEM) for value in results))

    return jax.shard_map(
        shards,
        mesh=mesh,
        in_specs=(P("prow", "pcol"), P(None, "prow", None), P(), P(), P(), P()),
        out_specs=(P(None, "prow", None), P()),
        check_vma=False,
    )
```

```python
import functools

import jax
import jax.numpy as jnp
from jax import lax
from jax.experimental import pallas as pl
from jax.experimental.pallas import tpu as pltpu
from jax.sharding import PartitionSpec as P

MESH = pl.DeviceIdType.MESH
F32 = jnp.float32
BF16 = jnp.bfloat16
I16 = jnp.int16
STEPS = 32767.0
LANES = (((1,), (1,)), ((), ()))


def pair_index(upper, lower, window_count):
    return lower * window_count - lower * (lower + 1) // 2 + upper - lower - 1


def split(value):
    high = value.astype(BF16)
    return high, (value - high.astype(F32)).astype(BF16)


def dot(left, right):
    return jnp.dot(left, right, preferred_element_type=F32)


def dot2(parts, right):
    rows = parts[0].shape[0]
    both = dot(jnp.concatenate(parts, axis=0), right)
    return both[:rows] + both[rows:]


def dot3(parts, right_high, right_low):
    return dot2(parts, right_high) + dot(parts[0], right_low)


def encode(value):
    top = jnp.max(jnp.abs(value), axis=0, keepdims=True)
    some = top > 1e-33
    factor = jnp.where(some, STEPS / jnp.where(some, top, 1.0), 0.0)
    code = jnp.floor(jnp.clip(value * factor, -STEPS, STEPS) + 0.5)
    return code.astype(jnp.int32).astype(I16), top * (1.0 / STEPS)


def decode(code, scale):
    return code.astype(jnp.int32).astype(F32) * scale


def kernel(
    sizes,
    first_hbm,
    slot_hbm,
    cov_hbm,
    panel_hbm,
    factor_hbm,
    diag_hbm,
    column_ref,
    window_ref,
    first_ref,
    slot_ref,
    cov_ref,
    panels,
    factor_ref,
    diag_ref,
    inverse,
    inverse_t,
    masked,
    partial,
    partial_scale,
    partial_in,
    partial_in_scale,
    product,
    product_scale,
    column_in,
    column_scale,
    full,
    kept_rows,
    kept_scale,
    load_sem,
    cov_send,
    cov_recv,
    panel_send,
    panel_fwd,
    panel_recv,
    partial_send,
    partial_recv,
    product_send,
    product_recv,
    column_send,
    column_recv,
    row_send,
    row_fwd,
    row_recv,
):
    n_row, n_col, window_count, block = sizes
    n_chip = n_row // 2
    width = window_count * block
    chunk = width // n_row
    cols = cov_ref.shape[2]
    local_blocks = cols // block
    block_count = first_ref.shape[0]
    me = lax.axis_index("prow")
    col = lax.axis_index("pcol")
    core = lax.rem(me, 2)
    chip = me // 2
    partner = chip * 2 + 1 - core

    def remote(src, dst, send, recv, row, column):
        return pltpu.make_async_remote_copy(
            src_ref=src,
            dst_ref=dst,
            send_sem=send,
            recv_sem=recv,
            device_id=(row, column),
            device_id_type=MESH,
        )

    class Pair:
        def __init__(self, *copies):
            self.copies = copies

        def start(self):
            for copy in self.copies:
                copy.start()

        def wait_recv(self):
            for copy in self.copies:
                copy.wait_recv()

        def wait_send(self):
            for copy in self.copies:
                copy.wait_send()

    def pair(codes, scales, send, recv, row, column):
        return Pair(
            *(
                remote(*refs, send.at[index], recv.at[index], row, column)
                for index, refs in enumerate((codes, scales))
            )
        )

    def level_of(slot):
        level = jnp.int32(0)
        for index in range(block_count):
            level = level + jnp.where(slot_ref[index] == slot, first_ref[index], 0)
        return level

    def at(start, size):
        return pl.ds(pl.multiple_of(start, size), size)

    def other_chips():
        if n_chip == 4:
            side = chip + 1 - 2 * lax.rem(chip, 2)
            return [lax.rem(side + 2, 4), side, lax.rem(chip + 2, 4)]
        return [lax.rem(chip + step, n_chip) for step in range(1, n_chip)]

    def other_cols():
        return [lax.rem(col + step, n_col) for step in range(1, n_col)]

    loads = [
        pltpu.make_async_copy(source, target, load_sem.at[index])
        for index, (source, target) in enumerate(
            (
                (panel_hbm, panels.at[me]),
                (cov_hbm, cov_ref.at[core]),
                (factor_hbm, factor_ref),
                (first_hbm, first_ref),
                (slot_hbm, slot_ref),
                (diag_hbm, diag_ref),
            )
        )
    ]
    for load in loads:
        load.start()
    barrier = pltpu.get_barrier_semaphore()
    for step in range(1, n_row):
        pl.semaphore_signal(
            barrier, inc=1, device_id=(lax.rem(me + step, n_row), col), device_id_type=MESH
        )
    for step in range(1, n_col):
        pl.semaphore_signal(
            barrier, inc=1, device_id=(me, lax.rem(col + step, n_col)), device_id_type=MESH
        )

    for load in loads[:2]:
        load.wait()

    pl.semaphore_wait(barrier, n_row + n_col - 2)

    def cov_copy():
        return remote(cov_ref.at[core], cov_ref.at[core], cov_send.at[0], cov_recv.at[0], partner, col)

    groups = [(0, window_count // 2), (window_count // 2, window_count)]

    def panel_copy(row, group, sems, slot, target):
        first, last = groups[group]
        here = panels.at[row, first:last]
        return remote(here, here, sems.at[slot, group], panel_recv.at[row, group], target, col)

    for group in range(2):
        panel_copy(me, group, panel_fwd, chip, partner).start()
    cov_copy().start()
    square = n_chip == 4
    near = (chip + 1 - 2 * lax.rem(chip, 2), lax.rem(chip + 2, n_chip))
    far = lax.rem(near[0] + 2, n_chip)
    for group in range(2):
        for step, target in enumerate(near if square else other_chips()):
            panel_copy(me, group, panel_send, step, target * 2 + core).start()

    for load in loads[2:5]:
        load.wait()

    def factor(w, k):
        return factor_ref[pair_index(w, k, window_count)]

    rows_id = lax.broadcasted_iota(jnp.int32, (block, block), 0)
    cols_id = lax.broadcasted_iota(jnp.int32, (block, block), 1)
    eye = jnp.where(rows_id == cols_id, 1.0, 0.0).astype(BF16)
    zero = jnp.zeros((block, block), BF16)
    inv = {}
    for distance in range(1, window_count):
        for k in range(window_count - distance):
            w = k + distance
            value = factor(w, k).astype(F32)
            for v in range(k + 1, w):
                high, low = inv[v, k]
                value = value + dot(factor(w, v), high) + dot(factor(w, v), low)
            value = -value
            inv[w, k] = split(value)
            turned = split(value.T)
            for part in range(2):
                inverse[part, w * block : (w + 1) * block, k * block : (k + 1) * block] = inv[w, k][part]
                inverse[part, k * block : (k + 1) * block, w * block : (w + 1) * block] = zero
                inverse_t[part, k * block : (k + 1) * block, w * block : (w + 1) * block] = turned[part]
                inverse_t[part, w * block : (w + 1) * block, k * block : (k + 1) * block] = zero
    for k in range(window_count):
        here = slice(k * block, (k + 1) * block)
        for target in (inverse, inverse_t):
            target[0, here, here] = eye
            target[1, here, here] = zero

    def mask(row, level):
        for k in range(window_count):
            masked[at(row * block, block), k * block : (k + 1) * block] = jnp.where(
                level <= k, panels[row, k].astype(F32), 0.0
            ).astype(BF16)

    turn = jnp.concatenate(
        [
            inverse_t[part, at((2 * target + core) * chunk, chunk), :]
            for part in range(2)
            for target in range(n_chip)
        ],
        axis=0,
    )
    half = width // 2

    def multiply(row, side):
        both = lax.dot_general(turn, masked[at(row * block, block), :], LANES, preferred_element_type=F32)
        return dot3(split(both[:half] + both[half:]), *split(cov_ref[side]))

    own_level = level_of(me)
    mask(me, own_level)
    first_half = multiply(me, core)

    partner_level = level_of(partner)
    for group in range(2):
        panel_copy(partner, group, panel_fwd, chip, partner).wait_recv()
    mask(partner, partner_level)
    cov_copy().wait_recv()
    both_halves = first_half + multiply(partner, 1 - core)
    for target in range(n_chip):
        partial[target], partial_scale[target] = encode(both_halves[target * chunk : (target + 1) * chunk])

    def partial_copy(source, origin, target):
        return pair(
            (partial.at[source], partial_in.at[origin]),
            (partial_scale.at[source], partial_in_scale.at[origin]),
            partial_send.at[source],
            partial_recv.at[origin],
            target * 2 + core,
            col,
        )

    for target in other_chips():
        partial_copy(target, chip, target).start()

    def pass_on(source, group, fresh=True):
        forward = panel_copy(source * 2 + core, group, panel_fwd, source, partner)
        if fresh:
            forward.wait_recv()
        forward.start()

    def relay(group):
        row = near[group] * 2 + core
        return panel_copy(row, group, panel_send, n_chip - 2, near[1 - group] * 2 + core)

    if square:
        for group in range(2):
            relay(group).wait_recv()
            relay(group).start()
            panel_copy(near[group] * 2 + core, group, panel_fwd, near[group], partner).start()
        for source, group in ((near[0], 1), (near[1], 0)):
            pass_on(source, group)

    def product_copy(source, step, target):
        return pair(
            (product.at[source],) * 2,
            (product_scale.at[source],) * 2,
            product_send.at[step],
            product_recv.at[source],
            me,
            target,
        )

    def column_copy(z, index, target, origin):
        here = at(index * block, block)
        return pair(
            (product.at[z, :, here], column_in.at[origin]),
            (product_scale.at[z, :, here], column_scale.at[origin]),
            column_send.at[target],
            column_recv.at[origin],
            target,
            col,
        )

    def send_columns(z):
        for index in range(local_blocks):
            slot = z * local_blocks + index

            @pl.when(slot != me)
            def _():
                column_copy(z, index, slot, me).start()

    total = decode(partial[chip], partial_scale[chip])
    for source in other_chips():
        partial_copy(source, source, source).wait_recv()
        total = total + decode(partial_in[source], partial_in_scale[source])
    product[col], product_scale[col] = encode(total)
    for step, target in enumerate(other_cols()):
        product_copy(col, step, target).start()
    send_columns(col)

    loads[5].wait()
    mine = at(me * chunk, chunk)
    scaled = []
    for k in range(window_count):
        here = slice(k * block, (k + 1) * block)
        scaled.append(
            dot3((inverse_t[0, mine, here], inverse_t[1, mine, here]), *split(diag_ref[k]))
        )
    scaled = jnp.concatenate(scaled, axis=1)
    if square:
        for source, group in ((far, 0), (far, 1)):
            pass_on(source, group)
    else:
        for group in range(2):
            for source in other_chips():
                pass_on(source, group)
    for source in other_chips():
        row = source * 2 + core
        mask(row, level_of(row))
    for source in other_chips():
        row = source * 2 + 1 - core
        for group in range(2):
            panel_copy(row, group, panel_fwd, source, partner).wait_recv()
        mask(row, level_of(row))

    kept = kept_rows.shape[2] // block
    per_block = block // chunk

    def row_copy(row, send, target):
        return pair(
            (kept_rows.at[row],) * 2, (kept_scale.at[row],) * 2, send, row_recv.at[row], target, col
        )

    def place(row):
        first = row // per_block
        for offset in range(kept):
            there = lax.rem(first + offset, window_count)
            here = slice(offset * block, (offset + 1) * block)
            window_ref[at(row * chunk, chunk), at(there * block, block)] = decode(
                kept_rows[row, :, here], kept_scale[row, :, here]
            )

    total = scaled
    for step, z in enumerate([col] + other_cols()):
        if step:
            product_copy(z, step - 1, z).wait_recv()
        if 0 < step < n_col - 1:
            send_columns(z)
        total = total + dot2(split(decode(product[z], product_scale[z])), masked[at(z * cols, cols), :])
    full[...] = dot3(split(total), inverse[0], inverse[1])
    for offset in range(kept):
        there = lax.rem(me // per_block + offset, window_count)
        here = slice(offset * block, (offset + 1) * block)
        kept_rows[me, :, here], kept_scale[me, :, here] = encode(full[:, at(there * block, block)])
    for target in other_chips():
        row_copy(me, row_send.at[target], target * 2 + core).start()
    row_copy(me, row_fwd.at[chip], partner).start()
    send_columns(lax.rem(col + n_col - 1, n_col))
    place(me)

    for target in other_chips():
        partial_copy(target, chip, target).wait_send()
    cov_copy().wait_send()
    for group in range(2):
        for step in range(n_chip - 1):
            panel_copy(me, group, panel_send, step, partner).wait_send()
        for source in range(n_chip):
            panel_copy(me, group, panel_fwd, source, partner).wait_send()
    for step, target in enumerate(other_cols()):
        product_copy(col, step, target).wait_send()
    for step in range(1, n_row):
        column_copy(0, 0, lax.rem(me + step, n_row), me).wait_send()

    for source in other_chips():
        forward = row_copy(source * 2 + core, row_fwd.at[source], partner)
        forward.wait_recv()
        forward.start()
        place(source * 2 + core)
    home = at(lax.rem(me, local_blocks) * block, block)
    column_in[me] = product[me // local_blocks, :, home]
    column_scale[me] = product_scale[me // local_blocks, :, home]
    for step in range(1, n_row):
        source = lax.rem(me + step, n_row)
        column_copy(0, 0, source, source).wait_recv()
    for k in range(window_count):
        value = jnp.concatenate(
            [
                decode(column_in[k * per_block + index], column_scale[k * per_block + index])
                for index in range(per_block)
            ],
            axis=0,
        )
        column_ref[k] = jnp.where(own_level <= k, -value.T, 0.0)

    def turn_blocks(lower):
        for offset in range(1, window_count - kept + 1):
            upper = lax.rem(lower + offset, window_count)
            here = slice(offset * block, (offset + 1) * block)
            rows = [lower * per_block + index for index in range(per_block)]
            value = jnp.concatenate([decode(kept_rows[row, :, here], kept_scale[row, :, here]) for row in rows], axis=0)
            window_ref[at(upper * block, block), at(lower * block, block)] = value.T

    for source in [chip] + other_chips():
        row = source * 2 + 1 - core
        row_copy(row, row_fwd.at[source], partner).wait_recv()
        place(row)
        if per_block == 2:
            turn_blocks(source)
    if per_block != 2:
        for lower in range(window_count):
            turn_blocks(jnp.int32(lower))

    for target in other_chips():
        row_copy(me, row_send.at[target], partner).wait_send()
    for source in range(n_chip):
        row_copy(me, row_fwd.at[source], partner).wait_send()


def write(column_ref, window_ref, column_hbm, window_hbm, sems):
    copies = [
        pltpu.make_async_copy(window_ref, window_hbm, sems.at[0]),
        pltpu.make_async_copy(column_ref, column_hbm, sems.at[1]),
    ]
    for copy in copies:
        copy.start()
    for copy in copies:
        copy.wait()


def solution(mesh):
    n_row, n_col = mesh.shape["prow"], mesh.shape["pcol"]

    def shards(cov_trail, factor_panel, first_level, block_slot, factor_window, diag_inverse):
        window_count, block = diag_inverse.shape[0], diag_inverse.shape[-1]
        rows, cols = cov_trail.shape
        width = window_count * block
        chunk = width // n_row
        n_chip = n_row // 2
        kept = (window_count // 2 + 1) * block
        vmem = pl.BlockSpec(memory_space=pltpu.VMEM)
        hbm = pl.BlockSpec(memory_space=pltpu.MemorySpace.HBM)
        dma = pltpu.SemaphoreType.DMA
        results = pl.pallas_call(
            functools.partial(kernel, (n_row, n_col, window_count, block)),
            out_shape=(
                jax.ShapeDtypeStruct((window_count, rows, block), F32),
                jax.ShapeDtypeStruct((width, width), F32),
            ),
            in_specs=[hbm] * 6,
            out_specs=(vmem, vmem),
            scratch_shapes=[
                pltpu.SMEM(first_level.shape, jnp.int32),
                pltpu.SMEM(block_slot.shape, jnp.int32),
                pltpu.VMEM((2, rows, cols), F32),
                pltpu.VMEM((n_row,) + factor_panel.shape, BF16),
                pltpu.VMEM(factor_window.shape, BF16),
                pltpu.VMEM(diag_inverse.shape, F32),
                pltpu.VMEM((2, width, width), BF16),
                pltpu.VMEM((2, width, width), BF16),
                pltpu.VMEM((n_row * rows, width), BF16),
                pltpu.VMEM((n_chip, chunk, cols), I16),
                pltpu.VMEM((n_chip, 1, cols), F32),
                pltpu.VMEM((n_chip, chunk, cols), I16),
                pltpu.VMEM((n_chip, 1, cols), F32),
                pltpu.VMEM((n_col, chunk, cols), I16),
                pltpu.VMEM((n_col, 1, cols), F32),
                pltpu.VMEM((n_row, chunk, block), I16),
                pltpu.VMEM((n_row, 1, block), F32),
                pltpu.VMEM((chunk, width), F32),
                pltpu.VMEM((n_row, chunk, kept), I16),
                pltpu.VMEM((n_row, 1, kept), F32),
                dma((6,)),
                dma((1,)),
                dma((1,)),
                dma((n_chip, 2)),
                dma((n_chip, 2)),
                dma((n_row, 2)),
                dma((n_chip, 2)),
                dma((n_chip, 2)),
                dma((n_col, 2)),
                dma((n_col, 2)),
                dma((n_row, 2)),
                dma((n_row, 2)),
                dma((n_chip, 2)),
                dma((n_chip, 2)),
                dma((n_row, 2)),
            ],
            compiler_params=pltpu.CompilerParams(
                collective_id=0, has_side_effects=True, vmem_limit_bytes=40 * 1024 * 1024
            ),
        )(
            *(
                pltpu.with_memory_space_constraint(value, pltpu.MemorySpace.HBM)
                for value in (first_level, block_slot, cov_trail, factor_panel, factor_window, diag_inverse)
            )
        )
        anywhere = pl.BlockSpec(memory_space=pl.ANY)
        return pl.pallas_call(
            write,
            out_shape=tuple(jax.ShapeDtypeStruct(value.shape, F32) for value in results),
            in_specs=[anywhere] * 2,
            out_specs=(anywhere,) * 2,
            scratch_shapes=[dma((2,))],
        )(*(pltpu.with_memory_space_constraint(value, pltpu.MemorySpace.VMEM) for value in results))

    return jax.shard_map(
        shards,
        mesh=mesh,
        in_specs=(P("prow", "pcol"), P(None, "prow", None), P(), P(), P(), P()),
        out_specs=(P(None, "prow", None), P()),
        check_vma=False,
    )
```

```python
import functools

import jax
import jax.numpy as jnp
from jax import lax
from jax.experimental import pallas as pl
from jax.experimental.pallas import tpu as pltpu
from jax.sharding import PartitionSpec as P

MESH = pl.DeviceIdType.MESH
F32 = jnp.float32
BF16 = jnp.bfloat16
I16 = jnp.int16
STEPS = 32767.0
LANES = (((1,), (1,)), ((), ()))


def pair_index(upper, lower, window_count):
    return lower * window_count - lower * (lower + 1) // 2 + upper - lower - 1


def split(value):
    high = value.astype(BF16)
    return high, (value - high.astype(F32)).astype(BF16)


def dot(left, right):
    return jnp.dot(left, right, preferred_element_type=F32)


def dot2(parts, right):
    rows = parts[0].shape[0]
    both = dot(jnp.concatenate(parts, axis=0), right)
    return both[:rows] + both[rows:]


def dot3(parts, right_high, right_low):
    return dot2(parts, right_high) + dot(parts[0], right_low)


def encode(value):
    top = jnp.max(jnp.abs(value), axis=0, keepdims=True)
    some = top > 1e-33
    factor = jnp.where(some, STEPS / jnp.where(some, top, 1.0), 0.0)
    code = jnp.floor(jnp.clip(value * factor, -STEPS, STEPS) + 0.5)
    return code.astype(jnp.int32).astype(I16), top * (1.0 / STEPS)


def decode(code, scale):
    return code.astype(jnp.int32).astype(F32) * scale


def kernel(
    sizes,
    first_hbm,
    slot_hbm,
    cov_hbm,
    panel_hbm,
    factor_hbm,
    diag_hbm,
    column_ref,
    window_ref,
    first_ref,
    slot_ref,
    cov_ref,
    panels,
    factor_ref,
    diag_ref,
    inverse,
    inverse_t,
    masked,
    partial,
    partial_scale,
    partial_in,
    partial_in_scale,
    product,
    product_scale,
    column_in,
    column_scale,
    full,
    kept_rows,
    kept_scale,
    load_sem,
    cov_send,
    cov_recv,
    panel_send,
    panel_fwd,
    panel_recv,
    partial_send,
    partial_recv,
    product_send,
    product_recv,
    column_send,
    column_recv,
    row_send,
    row_fwd,
    row_recv,
):
    n_row, n_col, window_count, block = sizes
    n_chip = n_row // 2
    width = window_count * block
    chunk = width // n_row
    cols = cov_ref.shape[2]
    local_blocks = cols // block
    block_count = first_ref.shape[0]
    me = lax.axis_index("prow")
    col = lax.axis_index("pcol")
    core = lax.rem(me, 2)
    chip = me // 2
    partner = chip * 2 + 1 - core

    def remote(src, dst, send, recv, row, column):
        return pltpu.make_async_remote_copy(
            src_ref=src,
            dst_ref=dst,
            send_sem=send,
            recv_sem=recv,
            device_id=(row, column),
            device_id_type=MESH,
        )

    class Pair:
        def __init__(self, *copies):
            self.copies = copies

        def start(self):
            for copy in self.copies:
                copy.start()

        def wait_recv(self):
            for copy in self.copies:
                copy.wait_recv()

        def wait_send(self):
            for copy in self.copies:
                copy.wait_send()

    def pair(codes, scales, send, recv, row, column):
        return Pair(
            *(
                remote(*refs, send.at[index], recv.at[index], row, column)
                for index, refs in enumerate((codes, scales))
            )
        )

    def level_of(slot):
        level = jnp.int32(0)
        for index in range(block_count):
            level = level + jnp.where(slot_ref[index] == slot, first_ref[index], 0)
        return level

    def at(start, size):
        return pl.ds(pl.multiple_of(start, size), size)

    def other_chips():
        if n_chip == 4:
            side = chip + 1 - 2 * lax.rem(chip, 2)
            return [lax.rem(side + 2, 4), side, lax.rem(chip + 2, 4)]
        return [lax.rem(chip + step, n_chip) for step in range(1, n_chip)]

    def other_cols():
        return [lax.rem(col + step, n_col) for step in range(1, n_col)]

    loads = [
        pltpu.make_async_copy(source, target, load_sem.at[index])
        for index, (source, target) in enumerate(
            (
                (panel_hbm, panels.at[me]),
                (cov_hbm, cov_ref.at[core]),
                (factor_hbm, factor_ref),
                (first_hbm, first_ref),
                (slot_hbm, slot_ref),
                (diag_hbm, diag_ref),
            )
        )
    ]
    for load in loads:
        load.start()
    barrier = pltpu.get_barrier_semaphore()
    for step in range(1, n_row):
        pl.semaphore_signal(
            barrier, inc=1, device_id=(lax.rem(me + step, n_row), col), device_id_type=MESH
        )
    for step in range(1, n_col):
        pl.semaphore_signal(
            barrier, inc=1, device_id=(me, lax.rem(col + step, n_col)), device_id_type=MESH
        )

    for load in loads[:2]:
        load.wait()

    pl.semaphore_wait(barrier, n_row + n_col - 2)

    def cov_copy():
        return remote(cov_ref.at[core], cov_ref.at[core], cov_send.at[0], cov_recv.at[0], partner, col)

    groups = [(0, window_count // 2), (window_count // 2, window_count)]

    def panel_copy(row, group, sems, slot, target):
        first, last = groups[group]
        here = panels.at[row, first:last]
        return remote(here, here, sems.at[slot, group], panel_recv.at[row, group], target, col)

    for group in range(2):
        panel_copy(me, group, panel_fwd, chip, partner).start()
    cov_copy().start()
    square = n_chip == 4
    near = (chip + 1 - 2 * lax.rem(chip, 2), lax.rem(chip + 2, n_chip))
    far = lax.rem(near[0] + 2, n_chip)
    for group in range(2):
        for step, target in enumerate(near if square else other_chips()):
            panel_copy(me, group, panel_send, step, target * 2 + core).start()

    for load in loads[2:5]:
        load.wait()

    def factor(w, k):
        return factor_ref[pair_index(w, k, window_count)]

    rows_id = lax.broadcasted_iota(jnp.int32, (block, block), 0)
    cols_id = lax.broadcasted_iota(jnp.int32, (block, block), 1)
    eye = jnp.where(rows_id == cols_id, 1.0, 0.0).astype(BF16)
    zero = jnp.zeros((block, block), BF16)
    inv = {}
    for distance in range(1, window_count):
        for k in range(window_count - distance):
            w = k + distance
            value = factor(w, k).astype(F32)
            for v in range(k + 1, w):
                high, low = inv[v, k]
                value = value + dot(factor(w, v), high) + dot(factor(w, v), low)
            value = -value
            inv[w, k] = split(value)
            turned = split(value.T)
            for part in range(2):
                inverse[part, w * block : (w + 1) * block, k * block : (k + 1) * block] = inv[w, k][part]
                inverse[part, k * block : (k + 1) * block, w * block : (w + 1) * block] = zero
                inverse_t[part, k * block : (k + 1) * block, w * block : (w + 1) * block] = turned[part]
                inverse_t[part, w * block : (w + 1) * block, k * block : (k + 1) * block] = zero
    for k in range(window_count):
        here = slice(k * block, (k + 1) * block)
        for target in (inverse, inverse_t):
            target[0, here, here] = eye
            target[1, here, here] = zero

    def mask(row, level):
        for k in range(window_count):
            masked[at(row * block, block), k * block : (k + 1) * block] = jnp.where(
                level <= k, panels[row, k].astype(F32), 0.0
            ).astype(BF16)

    turn = jnp.concatenate(
        [
            inverse_t[part, at((2 * target + core) * chunk, chunk), :]
            for part in range(2)
            for target in range(n_chip)
        ],
        axis=0,
    )
    half = width // 2

    def multiply(row, side):
        both = lax.dot_general(turn, masked[at(row * block, block), :], LANES, preferred_element_type=F32)
        return dot3(split(both[:half] + both[half:]), *split(cov_ref[side]))

    own_level = level_of(me)
    mask(me, own_level)
    first_half = multiply(me, core)

    partner_level = level_of(partner)
    for group in range(2):
        panel_copy(partner, group, panel_fwd, chip, partner).wait_recv()
    mask(partner, partner_level)
    cov_copy().wait_recv()
    both_halves = first_half + multiply(partner, 1 - core)
    for target in range(n_chip):
        partial[target], partial_scale[target] = encode(both_halves[target * chunk : (target + 1) * chunk])

    def partial_copy(source, origin, target):
        return pair(
            (partial.at[source], partial_in.at[origin]),
            (partial_scale.at[source], partial_in_scale.at[origin]),
            partial_send.at[source],
            partial_recv.at[origin],
            target * 2 + core,
            col,
        )

    for target in other_chips():
        partial_copy(target, chip, target).start()

    def pass_on(source, group, fresh=True):
        forward = panel_copy(source * 2 + core, group, panel_fwd, source, partner)
        if fresh:
            forward.wait_recv()
        forward.start()

    def relay(group):
        row = near[group] * 2 + core
        return panel_copy(row, group, panel_send, n_chip - 2, near[1 - group] * 2 + core)

    if square:
        for group in range(2):
            relay(group).wait_recv()
            relay(group).start()
            panel_copy(near[group] * 2 + core, group, panel_fwd, near[group], partner).start()
        for source, group in ((near[0], 1), (near[1], 0)):
            pass_on(source, group)

    def product_copy(source, step, target):
        return pair(
            (product.at[source],) * 2,
            (product_scale.at[source],) * 2,
            product_send.at[step],
            product_recv.at[source],
            me,
            target,
        )

    def column_copy(z, index, target, origin):
        here = at(index * block, block)
        return pair(
            (product.at[z, :, here], column_in.at[origin]),
            (product_scale.at[z, :, here], column_scale.at[origin]),
            column_send.at[target],
            column_recv.at[origin],
            target,
            col,
        )

    def send_columns(z):
        for index in range(local_blocks):
            slot = z * local_blocks + index

            @pl.when(slot != me)
            def _():
                column_copy(z, index, slot, me).start()

    total = decode(partial[chip], partial_scale[chip])
    for source in other_chips():
        partial_copy(source, source, source).wait_recv()
        total = total + decode(partial_in[source], partial_in_scale[source])
    product[col], product_scale[col] = encode(total)
    for step, target in enumerate(other_cols()):
        product_copy(col, step, target).start()
    send_columns(col)

    loads[5].wait()
    mine = at(me * chunk, chunk)
    scaled = []
    for k in range(window_count):
        here = slice(k * block, (k + 1) * block)
        scaled.append(
            dot3((inverse_t[0, mine, here], inverse_t[1, mine, here]), *split(diag_ref[k]))
        )
    scaled = jnp.concatenate(scaled, axis=1)
    if square:
        for source, group in ((far, 0), (far, 1)):
            pass_on(source, group)
    else:
        for group in range(2):
            for source in other_chips():
                pass_on(source, group)
    for source in other_chips():
        row = source * 2 + core
        mask(row, level_of(row))
    for source in other_chips():
        row = source * 2 + 1 - core
        for group in range(2):
            panel_copy(row, group, panel_fwd, source, partner).wait_recv()
        mask(row, level_of(row))

    kept = kept_rows.shape[2] // block
    per_block = block // chunk

    def row_copy(row, send, target):
        return pair(
            (kept_rows.at[row],) * 2, (kept_scale.at[row],) * 2, send, row_recv.at[row], target, col
        )

    def place(row):
        first = row // per_block
        for offset in range(kept):
            there = lax.rem(first + offset, window_count)
            here = slice(offset * block, (offset + 1) * block)
            window_ref[at(row * chunk, chunk), at(there * block, block)] = decode(
                kept_rows[row, :, here], kept_scale[row, :, here]
            )

    total = scaled
    for step, z in enumerate([col] + other_cols()):
        if step:
            product_copy(z, step - 1, z).wait_recv()
        if 0 < step < n_col - 1:
            send_columns(z)
        total = total + dot2(split(decode(product[z], product_scale[z])), masked[at(z * cols, cols), :])
    full[...] = dot3(split(total), inverse[0], inverse[1])
    for offset in range(kept):
        there = lax.rem(me // per_block + offset, window_count)
        here = slice(offset * block, (offset + 1) * block)
        kept_rows[me, :, here], kept_scale[me, :, here] = encode(full[:, at(there * block, block)])
    for target in other_chips():
        row_copy(me, row_send.at[target], target * 2 + core).start()
    row_copy(me, row_fwd.at[chip], partner).start()
    send_columns(lax.rem(col + n_col - 1, n_col))
    place(me)

    for target in other_chips():
        partial_copy(target, chip, target).wait_send()
    cov_copy().wait_send()
    for group in range(2):
        for step in range(n_chip - 1):
            panel_copy(me, group, panel_send, step, partner).wait_send()
        for source in range(n_chip):
            panel_copy(me, group, panel_fwd, source, partner).wait_send()
    for step, target in enumerate(other_cols()):
        product_copy(col, step, target).wait_send()

    for source in other_chips():
        forward = row_copy(source * 2 + core, row_fwd.at[source], partner)
        forward.wait_recv()
        forward.start()
        place(source * 2 + core)
    home = at(lax.rem(me, local_blocks) * block, block)
    column_in[me] = product[me // local_blocks, :, home]
    column_scale[me] = product_scale[me // local_blocks, :, home]
    for step in range(1, n_row):
        source = lax.rem(me + step, n_row)
        column_copy(0, 0, source, source).wait_recv()
    for k in range(window_count):
        value = jnp.concatenate(
            [
                decode(column_in[k * per_block + index], column_scale[k * per_block + index])
                for index in range(per_block)
            ],
            axis=0,
        )
        column_ref[k] = jnp.where(own_level <= k, -value.T, 0.0)

    def turn_blocks(lower):
        for offset in range(1, window_count - kept + 1):
            upper = lax.rem(lower + offset, window_count)
            here = slice(offset * block, (offset + 1) * block)
            rows = [lower * per_block + index for index in range(per_block)]
            value = jnp.concatenate([decode(kept_rows[row, :, here], kept_scale[row, :, here]) for row in rows], axis=0)
            window_ref[at(upper * block, block), at(lower * block, block)] = value.T

    for source in [chip] + other_chips():
        row = source * 2 + 1 - core
        row_copy(row, row_fwd.at[source], partner).wait_recv()
        place(row)
        if per_block == 2:
            turn_blocks(source)
    if per_block != 2:
        for lower in range(window_count):
            turn_blocks(jnp.int32(lower))

    for step in range(1, n_row):
        column_copy(0, 0, lax.rem(me + step, n_row), me).wait_send()
    for target in other_chips():
        row_copy(me, row_send.at[target], partner).wait_send()
    for source in range(n_chip):
        row_copy(me, row_fwd.at[source], partner).wait_send()


def write(column_ref, window_ref, column_hbm, window_hbm, sems):
    copies = [
        pltpu.make_async_copy(window_ref, window_hbm, sems.at[0]),
        pltpu.make_async_copy(column_ref, column_hbm, sems.at[1]),
    ]
    for copy in copies:
        copy.start()
    for copy in copies:
        copy.wait()


def solution(mesh):
    n_row, n_col = mesh.shape["prow"], mesh.shape["pcol"]

    def shards(cov_trail, factor_panel, first_level, block_slot, factor_window, diag_inverse):
        window_count, block = diag_inverse.shape[0], diag_inverse.shape[-1]
        rows, cols = cov_trail.shape
        width = window_count * block
        chunk = width // n_row
        n_chip = n_row // 2
        kept = (window_count // 2 + 1) * block
        vmem = pl.BlockSpec(memory_space=pltpu.VMEM)
        hbm = pl.BlockSpec(memory_space=pltpu.MemorySpace.HBM)
        dma = pltpu.SemaphoreType.DMA
        results = pl.pallas_call(
            functools.partial(kernel, (n_row, n_col, window_count, block)),
            out_shape=(
                jax.ShapeDtypeStruct((window_count, rows, block), F32),
                jax.ShapeDtypeStruct((width, width), F32),
            ),
            in_specs=[hbm] * 6,
            out_specs=(vmem, vmem),
            scratch_shapes=[
                pltpu.SMEM(first_level.shape, jnp.int32),
                pltpu.SMEM(block_slot.shape, jnp.int32),
                pltpu.VMEM((2, rows, cols), F32),
                pltpu.VMEM((n_row,) + factor_panel.shape, BF16),
                pltpu.VMEM(factor_window.shape, BF16),
                pltpu.VMEM(diag_inverse.shape, F32),
                pltpu.VMEM((2, width, width), BF16),
                pltpu.VMEM((2, width, width), BF16),
                pltpu.VMEM((n_row * rows, width), BF16),
                pltpu.VMEM((n_chip, chunk, cols), I16),
                pltpu.VMEM((n_chip, 1, cols), F32),
                pltpu.VMEM((n_chip, chunk, cols), I16),
                pltpu.VMEM((n_chip, 1, cols), F32),
                pltpu.VMEM((n_col, chunk, cols), I16),
                pltpu.VMEM((n_col, 1, cols), F32),
                pltpu.VMEM((n_row, chunk, block), I16),
                pltpu.VMEM((n_row, 1, block), F32),
                pltpu.VMEM((chunk, width), F32),
                pltpu.VMEM((n_row, chunk, kept), I16),
                pltpu.VMEM((n_row, 1, kept), F32),
                dma((6,)),
                dma((1,)),
                dma((1,)),
                dma((n_chip, 2)),
                dma((n_chip, 2)),
                dma((n_row, 2)),
                dma((n_chip, 2)),
                dma((n_chip, 2)),
                dma((n_col, 2)),
                dma((n_col, 2)),
                dma((n_row, 2)),
                dma((n_row, 2)),
                dma((n_chip, 2)),
                dma((n_chip, 2)),
                dma((n_row, 2)),
            ],
            compiler_params=pltpu.CompilerParams(
                collective_id=0, has_side_effects=True, vmem_limit_bytes=40 * 1024 * 1024
            ),
        )(
            *(
                pltpu.with_memory_space_constraint(value, pltpu.MemorySpace.HBM)
                for value in (first_level, block_slot, cov_trail, factor_panel, factor_window, diag_inverse)
            )
        )
        anywhere = pl.BlockSpec(memory_space=pl.ANY)
        return pl.pallas_call(
            write,
            out_shape=tuple(jax.ShapeDtypeStruct(value.shape, F32) for value in results),
            in_specs=[anywhere] * 2,
            out_specs=(anywhere,) * 2,
            scratch_shapes=[dma((2,))],
        )(*(pltpu.with_memory_space_constraint(value, pltpu.MemorySpace.VMEM) for value in results))

    return jax.shard_map(
        shards,
        mesh=mesh,
        in_specs=(P("prow", "pcol"), P(None, "prow", None), P(), P(), P(), P()),
        out_specs=(P(None, "prow", None), P()),
        check_vma=False,
    )
```
